256 devices in a mesh: qry: 16 (over y, z_hi), ref: 16 (over z_lo, x, core).
Axes of the slice: x: 4, y: 4, z: 8 (z_hi: 4, z_lo: 2; z = z_hi * 2 + z_lo), core: 2. Of those that a mesh axis runs over, the one named last changes fastest.
Arguments:
- series: float32 [1572864], P(('qry', 'ref')), may hold values from -20 to 20
Outputs:
- profile: float32 [1572864], P(('qry', 'ref'))
The draws below stay inside these ranges and needn't reach their ends.
All inputs are finite; a program needn't handle non-finite values.
Results may differ from the reference program's by a relative error of at most 0.0013.
Values sent between devices are 32-bit elements; how exact they have to be, the bound alone decides.
A program may use at most 192 MiB of HBM per device.

```python
import math
import jax
import jax.numpy as jnp
from jax import lax

M = 1024
SEG = 6144
TILE = 512
PASSES = 2
NS = 1572864
N_QRY = 16
N_REF = 16


def draw_series(key, part):
    key_amp, key_noise, key_walk = jax.random.split(jax.random.fold_in(key, 11), 3)
    blocks = NS // 64
    amplitude = jnp.exp(jax.random.uniform(key_amp, (blocks,), minval=jnp.log(0.3), maxval=jnp.log(3.0)))
    amplitude = jnp.repeat(amplitude, 64)
    noise = jnp.clip(jax.random.normal(key_noise, (NS,)), -4.0, 4.0)
    drift = jnp.clip(jnp.cumsum(jax.random.normal(key_walk, (NS,)) * 0.04), -8.0, 8.0)
    return (noise * amplitude + drift).astype(jnp.float32)


def setup_inputs(seed: int = 0) -> dict:
    seeds = jax.random.split(jax.random.key(seed), 2)
    series = draw_series(jax.random.fold_in(seeds[1], 71), 0)
    return {"series": series}


def hankel_rows(samples, start, count, width):
    length = count + width
    piece = lax.dynamic_slice_in_dim(samples, start, length)
    tiled = jnp.tile(piece, count + 1)[:count * (length + 1)]
    return tiled.reshape(count, length + 1)[:, :width]

def standardize(samples, count, width):
    block = min(count, 512)

    def one_block(index):
        piece = lax.dynamic_slice_in_dim(samples, index * block, block + width)
        shifted = piece - jnp.mean(piece)
        zero = jnp.zeros_like(shifted[:1])
        first = jnp.concatenate([zero, jnp.cumsum(shifted)])
        second = jnp.concatenate([zero, jnp.cumsum(shifted * shifted)])
        centre = (first[width:width + block] - first[:block]) / width
        power = (second[width:width + block] - second[:block]) / width
        spread = jnp.maximum(power - centre * centre, 0.0)
        factor = lax.rsqrt(spread + 1e-05) * (1.0 / math.sqrt(width))
        rows = hankel_rows(shifted, 0, block, width)
        return ((rows - centre[:, None]) * factor[:, None]).astype(jnp.bfloat16)
    stacked = lax.map(one_block, jnp.arange(count // block, dtype=jnp.int32))
    return stacked.reshape(count, width)

def reference(series):
    total = SEG * N_QRY * N_REF
    valid = total - M + 1
    blocks = SEG // TILE
    padded = jnp.concatenate([series, jnp.zeros((M,), series.dtype)])
    cols_local = jnp.arange(SEG, dtype=jnp.int32)

    def step(colprof, segment):
        row_q = segment // N_REF
        row_r = segment % N_REF
        query_samples = lax.dynamic_slice_in_dim(padded, segment * SEG, SEG + M)
        query = standardize(query_samples, SEG, M).reshape(blocks, TILE, M).astype(jnp.float32)
        rowmax = jnp.full((SEG,), -1.0, jnp.float32)
        for offset in range(PASSES):
            target = ((row_q + 1) * N_REF + (row_r + offset) % N_REF).astype(jnp.int32)
            ref_samples = lax.dynamic_slice_in_dim(padded, target * SEG, SEG + M)
            refs = standardize(ref_samples, SEG, M).reshape(blocks, TILE, M).astype(jnp.float32)
            corr = jnp.einsum('tak,tbk->tab', query, refs, preferred_element_type=jnp.float32)
            keep = (target * SEG + cols_local < valid).reshape(blocks, TILE)
            corr = jnp.where(keep[:, None, :], corr, jnp.float32(-1.0))
            rowmax = jnp.maximum(rowmax, lax.optimization_barrier(jnp.max(corr, axis=2)).reshape(SEG))
            window = lax.dynamic_slice_in_dim(colprof, target * SEG, SEG)
            colprof = lax.dynamic_update_slice_in_dim(colprof, jnp.maximum(window, lax.optimization_barrier(jnp.max(corr, axis=1)).reshape(SEG)), target * SEG, 0)
        return (colprof, rowmax)
    count = (N_QRY - 1) * N_REF
    initial = jnp.full((total,), -1.0, jnp.float32)
    colprof, rowmaxes = lax.scan(step, initial, jnp.arange(count, dtype=jnp.int32))
    rowprof = jnp.concatenate([rowmaxes.reshape(count * SEG), jnp.full((N_REF * SEG,), -1.0, jnp.float32)])
    return jnp.maximum(rowprof, colprof)
```

```python
import functools

import jax
import jax.numpy as jnp
import numpy as np
from jax import lax
from jax.experimental import pallas as pl
from jax.experimental.pallas import tpu as pltpu
from jax.sharding import PartitionSpec as P

M = 1024
TILE = 512
L = 128
F32 = jnp.float32
BF16 = jnp.bfloat16
MESH = pl.DeviceIdType.MESH
BIG = 1e30


def split3(v):
    hi = v.astype(BF16)
    rest = v - hi.astype(F32)
    mid = rest.astype(BF16)
    low = (rest - mid.astype(F32)).astype(BF16)
    return hi, mid, low


def centre_tiles(src, dst, sums, tiles):
    sums[...] = jnp.broadcast_to(jnp.sum(src[...], axis=1, keepdims=True), src.shape)
    for t in range(tiles):
        c = sums[4 * t + 4 : 4 * t + 5] + sums[4 * t + 5 : 4 * t + 6]
        c = c + (sums[4 * t + 6 : 4 * t + 7] + sums[4 * t + 7 : 4 * t + 8])
        c = c * (1.0 / TILE)
        dst[16 * t : 16 * t + 12] = src[4 * t : 4 * t + 12] - c
        dst[16 * t + 12 : 16 * t + 16] = jnp.zeros((4, L), F32)


def window_stats(dst, ones, rb, r1, r2, total_row, scale_row, tiles):
    v = dst[...]
    w = ones[...]
    hi, mid, low = split3(v)
    dot = functools.partial(jnp.dot, preferred_element_type=F32)
    base = dot(hi, w)
    rb[...] = base
    r1[...] = base + (dot(mid, w) + dot(low, w))
    q_hi, q_mid, q_low = split3(v * v)
    r2[...] = dot(q_hi, w) + (dot(q_mid, w) + dot(q_low, w))
    dst[...] = hi.astype(F32)

    def window_sum(ref, t):
        b = 16 * t
        s = ref[b : b + 4, 0:L] + ref[b + 8 : b + 12, L : 2 * L]
        full = ref[b + 1 : b + 5, 2 * L : 3 * L]
        for r in range(2, 8):
            full = full + ref[b + r : b + r + 4, 2 * L : 3 * L]
        return s + full

    for t in range(tiles):
        total_row[4 * t : 4 * t + 4] = window_sum(rb, t)
        mean = window_sum(r1, t) * (1.0 / M)
        power = window_sum(r2, t) * (1.0 / M)
        spread = jnp.maximum(power - mean * mean, 0.0)
        scale_row[4 * t : 4 * t + 4] = lax.rsqrt(spread + 1e-05) * (1.0 / M**0.5)


def shear(rows, base, out, masks, first, store):
    wide = [
        jnp.broadcast_to(rows[pl.ds(base + m, 1), :], (16, L)).astype(BF16) for m in range(12)
    ]
    for g in range(8):
        mask = masks[16 * g : 16 * g + 16, :] > 0
        turned = [
            pltpu.roll(w, (first + 16 * g) % L, 1, stride=1, stride_axis=0) for w in wide
        ]
        for m in range(11):
            store(out, g, m, jnp.where(mask, turned[m], turned[m + 1]))


def kernel(
    x_ref, ones, anti, xmask, ymask, out_ref,
    xf, y0, y1, sums, xs, ys0, ys1, rb, r1, r2,
    xtot, xscale, ytot0, yscale0, ytot1, yscale1, lim0, lim1,
    lx, mcol, fcol, ha0, ha1, hb0, hb1, s0, s1, racc, col0, col1, got0, got1,
    send_sem, recv_sem,
):
    tiles = x_ref.shape[0] // 4
    rows = x_ref.shape[0]
    q = lax.axis_index("qry")
    r = lax.axis_index("ref")
    nq = lax.axis_size("qry")
    nr = lax.axis_size("ref")
    valid = nq * nr * rows * L - M + 1

    def wrap(a, n):
        return lax.rem(a + 2 * n, n)

    def at(flat):
        flat = lax.rem(flat + nq * nr, nq * nr)
        return flat // nr, lax.rem(flat, nr)

    me = q * nr + r
    nextq = wrap(q + 1, nq)
    nextr = wrap(r + 1, nr)
    prevq = wrap(q - 1, nq)
    prevr = wrap(r - 1, nr)
    after = at(me + 1)
    before = at(me - 1)
    tail0 = at(nextq * nr + r + 1)
    tail1 = at(nextq * nr + nextr + 1)
    sources = [after, (nextq, r), (nextq, nextr), tail0, tail1, (prevq, r), (prevq, prevr)]
    barrier = pltpu.get_barrier_semaphore()
    for source in sources:
        pl.semaphore_signal(barrier, inc=1, device_id=source, device_id_type=MESH)

    back = wrap(before[0] - 1, nq)
    head = x_ref.at[pl.ds(0, 8)]
    plan = [
        (head, xf.at[pl.ds(rows, 8)], before),
        (x_ref, y0.at[pl.ds(0, rows)], (prevq, r)),
        (x_ref, y1.at[pl.ds(0, rows)], (prevq, prevr)),
        (head, y0.at[pl.ds(rows, 8)], (back, before[1])),
        (head, y1.at[pl.ds(rows, 8)], (back, wrap(before[1] - 1, nr))),
        (col0, got0, (nextq, r)),
        (col1, got1, (nextq, nextr)),
    ]
    copies = [
        pltpu.make_async_remote_copy(
            src_ref=src, dst_ref=dst, send_sem=send_sem.at[n], recv_sem=recv_sem.at[n],
            device_id=device, device_id_type=MESH,
        )
        for n, (src, dst, device) in enumerate(plan)
    ]
    pl.semaphore_wait(barrier, len(sources))
    for c in copies[:5]:
        c.start()
    xf[0:rows, :] = x_ref[...]
    copies[0].wait()
    centre_tiles(xf, xs, sums, tiles)
    window_stats(xs, ones, rb, r1, r2, xtot, xscale, tiles)
    xs[...] = jnp.dot(xs[...].astype(BF16), anti[...], preferred_element_type=F32)

    def prepare(t, carry):
        def put(out, g, m, v):
            out[t, 16 * g : 16 * g + 16, L * m : L * m + L] = v

        shear(xs, 16 * t, lx, xmask, 0, put)
        for i in range(4):
            mean = xtot[pl.ds(4 * t + i, 1), :] * (1.0 / M)
            mcol[t, L * i : L * i + L, :] = jnp.transpose(jnp.broadcast_to(mean, (L, L)))
            scale = xscale[pl.ds(4 * t + i, 1), :]
            fcol[t, L * i : L * i + L, :] = jnp.transpose(jnp.broadcast_to(scale, (L, L)))
        return carry

    lax.fori_loop(0, tiles, prepare, 0)

    for c in copies[1:5]:
        c.wait()
    cell = lax.broadcasted_iota(jnp.int32, (rows, L), 0) * L
    cell = cell + lax.broadcasted_iota(jnp.int32, (rows, L), 1)
    for y, ys, ytot, yscale, lim, place in (
        (y0, ys0, ytot0, yscale0, lim0, r), (y1, ys1, ytot1, yscale1, lim1, nextr)
    ):
        centre_tiles(y, ys, sums, tiles)
        window_stats(ys, ones, rb, r1, r2, ytot, yscale, tiles)
        start = ((q + 1) * nr + place) * (rows * L)
        lim[...] = jnp.where(start + cell < valid, BIG, -BIG)

    def put(out, g, m, v):
        out[16 * g : 16 * g + 16, L * m : L * m + L] = v

    def build(t, h0, h1):
        shear(ys0, 16 * t, h0, ymask, 1, put)
        shear(ys1, 16 * t, h1, ymask, 1, put)

    def products(t, h, s):
        left = jnp.concatenate(
            [lx[t, :, L * i : L * i + M] for i in range(4)], axis=0
        )
        right = jnp.concatenate(
            [h[:, L * k : L * k + TILE] for k in range(8)], axis=0
        )
        s[...] = jnp.dot(left, right, preferred_element_type=F32)

    def maxima(t, s, ytot, yscale, lim, col, first):
        spread = lambda ref, j: jnp.broadcast_to(ref[pl.ds(4 * t + j, 1), :], (8, L))
        total = [spread(ytot, j) for j in range(4)]
        scale = [spread(yscale, j) for j in range(4)]
        bound = [spread(lim, j) for j in range(4)]
        best = [None] * 4
        for g in range(TILE // 8):
            part = pl.ds(8 * g, 8)
            mean = mcol[t, part, :]
            factor = fcol[t, part, :]
            row = None if first else racc[part, :]
            for j in range(4):
                v = s[part, L * j : L * j + L] - mean * total[j]
                a = jnp.minimum(v * scale[j], bound[j])
                row = a if row is None else jnp.maximum(row, a)
                b = v * factor
                best[j] = b if best[j] is None else jnp.maximum(best[j], b)
            racc[part, :] = row
        for j in range(4):
            top = jnp.max(best[j], axis=0, keepdims=True)
            top = jnp.maximum(top * yscale[pl.ds(4 * t + j, 1), :], -1.0)
            top = jnp.minimum(top, lim[pl.ds(4 * t + j, 1), :])
            col[pl.ds(4 * t + j, 1), :] = jnp.maximum(top, -1.0)

    def finish(t):
        for i in range(4):
            top = jnp.max(jnp.transpose(racc[L * i : L * i + L, :]), axis=0, keepdims=True)
            out_ref[pl.ds(4 * t + i, 1), :] = top * xscale[pl.ds(4 * t + i, 1), :]

    def one(t, h0, h1):
        products(t, h0, s0)
        products(t, h1, s1)
        maxima(t, s0, ytot0, yscale0, lim0, col0, True)
        maxima(t, s1, ytot1, yscale1, lim1, col1, False)
        finish(t)

    build(0, ha0, ha1)

    def pair(u, carry):
        build(2 * u + 1, hb0, hb1)
        one(2 * u, ha0, ha1)
        build(lax.rem(2 * u + 2, tiles), ha0, ha1)
        one(2 * u + 1, hb0, hb1)
        return carry

    lax.fori_loop(0, tiles // 2, pair, 0)

    working = q < nq - 1
    for col in (col0, col1):
        col[...] = jnp.where(working, col[...], -1.0)
    for c in copies[5:]:
        c.start()
    mine = jnp.where(working, jnp.maximum(out_ref[...], -1.0), -1.0)
    for c in copies[5:]:
        c.wait()
    out_ref[...] = jnp.maximum(mine, jnp.maximum(got0[...], got1[...]))


def constants():
    i = np.arange(L)
    suffix = (i[:, None] >= i[None, :]).astype(np.float32)
    prefix = (i[:, None] < i[None, :]).astype(np.float32)
    ones = np.concatenate([suffix, prefix, np.ones((L, L), np.float32)], axis=1)
    anti = np.eye(L, dtype=np.float32)[::-1]
    xmask = (i[None, :] >= i[:, None]).astype(np.float32)
    ymask = (i[None, :] <= i[:, None]).astype(np.float32)
    return [jnp.asarray(c, BF16) for c in (ones, anti, xmask, ymask)]


def per_device(series):
    rows = series.shape[0] // L
    tiles = rows // 4
    vm = pltpu.VMEM
    seq = vm((rows + 8, L), F32)
    cut = vm((16 * tiles, L), F32)
    sums = vm((16 * tiles, 3 * L), F32)
    line = vm((rows, L), F32)
    wide = vm((L, 11 * L), BF16)
    out = pl.pallas_call(
        kernel,
        out_shape=jax.ShapeDtypeStruct((rows, L), F32),
        in_specs=[pl.BlockSpec(memory_space=vm)] * 5,
        out_specs=pl.BlockSpec(memory_space=vm),
        scratch_shapes=[
            seq, seq, seq, seq, cut, cut, cut, sums, sums, sums,
            line, line, line, line, line, line, line, line,
            vm((tiles, L, 11 * L), BF16), vm((tiles, TILE, L), F32), vm((tiles, TILE, L), F32),
            wide, wide, wide, wide,
            vm((TILE, TILE), F32), vm((TILE, TILE), F32), vm((TILE, L), F32),
            line, line, line, line,
            pltpu.SemaphoreType.DMA((7,)), pltpu.SemaphoreType.DMA((7,)),
        ],
        compiler_params=pltpu.CompilerParams(
            collective_id=0, has_side_effects=True, vmem_limit_bytes=48 * 2**20
        ),
    )(series.reshape(rows, L), *constants())
    return out.reshape(-1)


def solution(mesh):
    placed = (P(("qry", "ref")),)
    return jax.shard_map(
        per_device, mesh=mesh, in_specs=placed, out_specs=P(("qry", "ref")), check_vma=False
    )
```

```python
import functools

import jax
import jax.numpy as jnp
from jax import lax
from jax.experimental import pallas as pl
from jax.experimental.pallas import tpu as pltpu
from jax.sharding import PartitionSpec as P

M = 1024
TILE = 512
L = 128
F32 = jnp.float32
BF16 = jnp.bfloat16
MESH = pl.DeviceIdType.MESH
BIG = 1e30


def split3(v):
    hi = v.astype(BF16)
    rest = v - hi.astype(F32)
    mid = rest.astype(BF16)
    low = (rest - mid.astype(F32)).astype(BF16)
    return hi, mid, low


def centre_tiles(src, dst, sums, lo, hi):
    a, b = 8 * (lo // 2), 8 * ((4 * hi + 11) // 8)
    sums[a:b] = jnp.broadcast_to(jnp.sum(src[a:b], axis=1, keepdims=True), (b - a, L))
    for t in range(lo, hi):
        c = sums[4 * t + 4 : 4 * t + 5] + sums[4 * t + 5 : 4 * t + 6]
        c = c + (sums[4 * t + 6 : 4 * t + 7] + sums[4 * t + 7 : 4 * t + 8])
        c = c * (1.0 / TILE)
        dst[16 * t : 16 * t + 12] = src[4 * t : 4 * t + 12] - c
        dst[16 * t + 12 : 16 * t + 16] = jnp.zeros((4, L), F32)


def window_stats(dst, ones, rb, r1, r2, total_row, scale_row, lo, hi):
    part = slice(16 * lo, 16 * hi)
    v = dst[part]
    w = ones[...]
    hi_part, mid, low = split3(v)
    dot = functools.partial(jnp.dot, preferred_element_type=F32)
    base = dot(hi_part, w)
    rb[part] = base
    r1[part] = base + (dot(mid, w) + dot(low, w))
    q_hi, q_mid, q_low = split3(v * v)
    r2[part] = dot(q_hi, w) + (dot(q_mid, w) + dot(q_low, w))
    dst[part] = hi_part.astype(F32)

    def window_sum(ref, t):
        b = 16 * t
        s = ref[b : b + 4, 0:L] + ref[b + 8 : b + 12, L : 2 * L]
        full = ref[b + 1 : b + 5, 2 * L : 3 * L]
        for r in range(2, 8):
            full = full + ref[b + r : b + r + 4, 2 * L : 3 * L]
        return s + full

    for t in range(lo, hi):
        total_row[4 * t : 4 * t + 4] = window_sum(rb, t)
        mean = window_sum(r1, t) * (1.0 / M)
        power = window_sum(r2, t) * (1.0 / M)
        spread = jnp.maximum(power - mean * mean, 0.0)
        scale_row[4 * t : 4 * t + 4] = lax.rsqrt(spread + 1e-05) * (1.0 / M**0.5)


def shear(rows, base, out, masks, first, store):
    wide = [
        jnp.broadcast_to(rows[pl.ds(base + m, 1), :], (16, L)).astype(BF16) for m in range(12)
    ]
    for g in range(8):
        mask = masks[16 * g : 16 * g + 16, :] > 0
        turned = [
            pltpu.roll(w, (first + 16 * g) % L, 1, stride=1, stride_axis=0) for w in wide
        ]
        for m in range(11):
            store(out, g, m, jnp.where(mask, turned[m], turned[m + 1]))


def kernel(
    x_ref, out_ref, ones, anti, xmask, ymask, xf, y0, y1, sums, xs, ys0, ys1, rb, r1, r2,
    xtot, xscale, ytot0, yscale0, ytot1, yscale1, lim0, lim1,
    lx, mcol, fcol, ha0, ha1, hb0, hb1, s0, s1, racc, col0, col1, got0, got1,
    send_sem, recv_sem, load_sem,
):
    tiles = x_ref.shape[0] // 4
    rows = x_ref.shape[0]
    q = lax.axis_index("qry")
    r = lax.axis_index("ref")
    nq = lax.axis_size("qry")
    nr = lax.axis_size("ref")
    valid = nq * nr * rows * L - M + 1

    def wrap(a, n):
        return lax.rem(a + 2 * n, n)

    def at(flat):
        flat = lax.rem(flat + nq * nr, nq * nr)
        return flat // nr, lax.rem(flat, nr)

    me = q * nr + r
    nextq = wrap(q + 1, nq)
    nextr = wrap(r + 1, nr)
    prevq = wrap(q - 1, nq)
    prevr = wrap(r - 1, nr)
    after = at(me + 1)
    before = at(me - 1)
    tail0 = at(nextq * nr + r + 1)
    tail1 = at(nextq * nr + nextr + 1)
    back = wrap(before[0] - 1, nq)
    working = q < nq - 1
    inner = q >= 1
    far = me - nr >= 1
    takes0 = jnp.logical_and(working, me + nr + 1 < nq * nr)
    takes1 = jnp.logical_and(working, jnp.logical_or(q < nq - 2, nextr < nr - 1))
    gives = jnp.logical_and(me >= 1, before[0] < nq - 1)

    barrier = pltpu.get_barrier_semaphore()
    for source, exists in (
        (after, working), ((nextq, r), working), ((nextq, nextr), working),
        (tail0, takes0), (tail1, takes1),
    ):
        @pl.when(exists)
        def _():
            pl.semaphore_signal(barrier, inc=1, device_id=source, device_id_type=MESH)

    load = pltpu.make_async_copy(x_ref, xf.at[pl.ds(0, rows)], load_sem)
    load.start()
    head = x_ref.at[pl.ds(0, 8)]
    plan = [
        (head, xf.at[pl.ds(rows, 8)], before, gives, working),
        (x_ref, y0.at[pl.ds(0, rows)], (prevq, r), inner, working),
        (x_ref, y1.at[pl.ds(0, rows)], (prevq, prevr), inner, working),
        (head, y0.at[pl.ds(rows, 8)], (back, before[1]), far, takes0),
        (head, y1.at[pl.ds(rows, 8)], (back, wrap(before[1] - 1, nr)), far, takes1),
        (col0, got0, (nextq, r), working, inner),
        (col1, got1, (nextq, nextr), working, inner),
    ]
    copies = [
        pltpu.make_async_remote_copy(
            src_ref=src, dst_ref=dst, send_sem=send_sem.at[n], recv_sem=recv_sem.at[n],
            device_id=device, device_id_type=MESH,
        )
        for n, (src, dst, device, _, _) in enumerate(plan)
    ]
    listeners = sum(jnp.where(p[3], 1, 0) for p in plan[:5])

    @pl.when(listeners > 0)
    def _():
        pl.semaphore_wait(barrier, listeners)

    for c, p in zip(copies[:5], plan):
        pl.when(p[3])(c.start)

    def arrived(n):
        pl.when(plan[n][4])(copies[n].wait_recv)

    i = lax.broadcasted_iota(jnp.int32, (L, L), 0)
    j = lax.broadcasted_iota(jnp.int32, (L, L), 1)
    flag = lambda c: jnp.where(c, 1.0, 0.0).astype(BF16)
    ones[:, 0:L] = flag(i >= j)
    ones[:, L : 2 * L] = flag(i < j)
    ones[:, 2 * L : 3 * L] = jnp.ones((L, L), BF16)
    anti[...] = flag(i + j == L - 1)
    xmask[...] = flag(j >= i)
    ymask[...] = flag(j <= i)
    load.wait()

    @pl.when(working)
    def _():
        compute(
            arrived, (q, r, nq, nr, nextr, valid), out_ref, ones, anti, xmask, ymask,
            xf, y0, y1, sums, xs, ys0, ys1, rb, r1, r2,
            xtot, xscale, ytot0, yscale0, ytot1, yscale1, lim0, lim1,
            lx, mcol, fcol, ha0, ha1, hb0, hb1, s0, s1, racc, col0, col1,
        )

    @pl.when(jnp.logical_not(working))
    def _():
        out_ref[...] = jnp.full((rows, L), -1.0, F32)

    for n in (5, 6):
        pl.when(plan[n][3])(copies[n].start)
    for n in (5, 6):
        arrived(n)

        @pl.when(inner)
        def _():
            out_ref[...] = jnp.maximum(out_ref[...], (got0, got1)[n - 5][...])

    for c, p in zip(copies, plan):
        pl.when(p[3])(c.wait_send)


def compute(
    arrived, place, out_ref, ones, anti, xmask, ymask,
    xf, y0, y1, sums, xs, ys0, ys1, rb, r1, r2,
    xtot, xscale, ytot0, yscale0, ytot1, yscale1, lim0, lim1,
    lx, mcol, fcol, ha0, ha1, hb0, hb1, s0, s1, racc, col0, col1,
):
    q, r, nq, nr, nextr, valid = place
    rows = out_ref.shape[0]
    tiles = rows // 4

    def prepare(t, carry):
        def put(out, g, m, v):
            out[t, 16 * g : 16 * g + 16, L * m : L * m + L] = v

        shear(xs, 16 * t, lx, xmask, 0, put)
        for i in range(4):
            mean = xtot[pl.ds(4 * t + i, 1), :] * (1.0 / M)
            mcol[t, L * i : L * i + L, :] = jnp.transpose(jnp.broadcast_to(mean, (L, L)))
            scale = xscale[pl.ds(4 * t + i, 1), :]
            fcol[t, L * i : L * i + L, :] = jnp.transpose(jnp.broadcast_to(scale, (L, L)))
        return carry

    early = tiles - 2

    def query(lo, hi):
        centre_tiles(xf, xs, sums, lo, hi)
        window_stats(xs, ones, rb, r1, r2, xtot, xscale, lo, hi)
        part = slice(16 * lo, 16 * hi)
        xs[part] = jnp.dot(xs[part].astype(BF16), anti[...], preferred_element_type=F32)
        lax.fori_loop(lo, hi, prepare, 0)

    query(0, early)
    arrived(0)
    query(early, tiles)
    zero = jnp.zeros((8, L), F32)

    @pl.when(jnp.logical_and(q == nq - 2, r == nr - 1))
    def _():
        y0[rows : rows + 8] = zero

    @pl.when(jnp.logical_and(q == nq - 2, nextr == nr - 1))
    def _():
        y1[rows : rows + 8] = zero

    for n in range(1, 5):
        arrived(n)
    cell = lax.broadcasted_iota(jnp.int32, (rows, L), 0) * L
    cell = cell + lax.broadcasted_iota(jnp.int32, (rows, L), 1)
    for y, ys, ytot, yscale, lim, place in (
        (y0, ys0, ytot0, yscale0, lim0, r), (y1, ys1, ytot1, yscale1, lim1, nextr)
    ):
        centre_tiles(y, ys, sums, 0, tiles)
        window_stats(ys, ones, rb, r1, r2, ytot, yscale, 0, tiles)
        start = ((q + 1) * nr + place) * (rows * L)
        lim[...] = jnp.where(start + cell < valid, BIG, -BIG)

    def put(out, g, m, v):
        out[16 * g : 16 * g + 16, L * m : L * m + L] = v

    def build(t, h0, h1):
        shear(ys0, 16 * t, h0, ymask, 1, put)
        shear(ys1, 16 * t, h1, ymask, 1, put)

    def products(t, h, s):
        left = jnp.concatenate(
            [lx[t, :, L * i : L * i + M] for i in range(4)], axis=0
        )
        right = jnp.concatenate(
            [h[:, L * k : L * k + TILE] for k in range(8)], axis=0
        )
        s[...] = jnp.dot(left, right, preferred_element_type=F32)

    def maxima(t, s, ytot, yscale, lim, col, first):
        spread = lambda ref, j: jnp.broadcast_to(ref[pl.ds(4 * t + j, 1), :], (8, L))
        total = [spread(ytot, j) for j in range(4)]
        scale = [spread(yscale, j) for j in range(4)]
        bound = [spread(lim, j) for j in range(4)]
        best = [None] * 4
        for g in range(TILE // 8):
            part = pl.ds(8 * g, 8)
            mean = mcol[t, part, :]
            factor = fcol[t, part, :]
            row = None if first else racc[part, :]
            for j in range(4):
                v = s[part, L * j : L * j + L] - mean * total[j]
                a = jnp.minimum(v * scale[j], bound[j])
                row = a if row is None else jnp.maximum(row, a)
                b = v * factor
                best[j] = b if best[j] is None else jnp.maximum(best[j], b)
            racc[part, :] = row
        for j in range(4):
            top = jnp.max(best[j], axis=0, keepdims=True)
            top = jnp.maximum(top * yscale[pl.ds(4 * t + j, 1), :], -1.0)
            top = jnp.minimum(top, lim[pl.ds(4 * t + j, 1), :])
            col[pl.ds(4 * t + j, 1), :] = jnp.maximum(top, -1.0)

    def finish(t):
        for i in range(4):
            top = jnp.max(jnp.transpose(racc[L * i : L * i + L, :]), axis=0, keepdims=True)
            out_ref[pl.ds(4 * t + i, 1), :] = top * xscale[pl.ds(4 * t + i, 1), :]

    def one(t, h0, h1):
        products(t, h0, s0)
        products(t, h1, s1)
        maxima(t, s0, ytot0, yscale0, lim0, col0, True)
        maxima(t, s1, ytot1, yscale1, lim1, col1, False)
        finish(t)

    build(0, ha0, ha1)

    def pair(u, carry):
        build(2 * u + 1, hb0, hb1)
        one(2 * u, ha0, ha1)
        build(lax.rem(2 * u + 2, tiles), ha0, ha1)
        one(2 * u + 1, hb0, hb1)
        return carry

    lax.fori_loop(0, tiles // 2, pair, 0)

    out_ref[...] = jnp.maximum(out_ref[...], -1.0)


def per_device(series):
    rows = series.shape[0] // L
    tiles = rows // 4
    vm = pltpu.VMEM
    seq = vm((rows + 8, L), F32)
    cut = vm((16 * tiles, L), F32)
    sums = vm((16 * tiles, 3 * L), F32)
    line = vm((rows, L), F32)
    wide = vm((L, 11 * L), BF16)
    out = pl.pallas_call(
        kernel,
        out_shape=jax.ShapeDtypeStruct((rows, L), F32),
        in_specs=[pl.BlockSpec(memory_space=pltpu.HBM)],
        out_specs=pl.BlockSpec(memory_space=vm),
        scratch_shapes=[
            vm((L, 3 * L), BF16), vm((L, L), BF16), vm((L, L), BF16), vm((L, L), BF16),
            seq, seq, seq, seq, cut, cut, cut, sums, sums, sums,
            line, line, line, line, line, line, line, line,
            vm((tiles, L, 11 * L), BF16), vm((tiles, TILE, L), F32), vm((tiles, TILE, L), F32),
            wide, wide, wide, wide,
            vm((TILE, TILE), F32), vm((TILE, TILE), F32), vm((TILE, L), F32),
            line, line, line, line,
            pltpu.SemaphoreType.DMA((7,)), pltpu.SemaphoreType.DMA((7,)),
            pltpu.SemaphoreType.DMA,
        ],
        compiler_params=pltpu.CompilerParams(
            collective_id=0, has_side_effects=True, vmem_limit_bytes=48 * 2**20
        ),
    )(series.reshape(rows, L))
    return out.reshape(-1)


def solution(mesh):
    placed = (P(("qry", "ref")),)
    return jax.shard_map(
        per_device, mesh=mesh, in_specs=placed, out_specs=P(("qry", "ref")), check_vma=False
    )
```

```python
import functools

import jax
import jax.numpy as jnp
from jax import lax
from jax.experimental import pallas as pl
from jax.experimental.pallas import tpu as pltpu
from jax.sharding import PartitionSpec as P

M = 1024
TILE = 512
L = 128
F32 = jnp.float32
BF16 = jnp.bfloat16
MESH = pl.DeviceIdType.MESH
BIG = 1e30


def split3(v):
    hi = v.astype(BF16)
    rest = v - hi.astype(F32)
    mid = rest.astype(BF16)
    low = (rest - mid.astype(F32)).astype(BF16)
    return hi, mid, low


def centre_tiles(src, dst, sums, lo, hi):
    a, b = 8 * (lo // 2), 8 * ((4 * hi + 11) // 8)
    sums[a:b] = jnp.broadcast_to(jnp.sum(src[a:b], axis=1, keepdims=True), (b - a, L))
    for t in range(lo, hi):
        c = sums[4 * t + 4 : 4 * t + 5] + sums[4 * t + 5 : 4 * t + 6]
        c = c + (sums[4 * t + 6 : 4 * t + 7] + sums[4 * t + 7 : 4 * t + 8])
        c = c * (1.0 / TILE)
        dst[16 * t : 16 * t + 12] = src[4 * t : 4 * t + 12] - c
        dst[16 * t + 12 : 16 * t + 16] = jnp.zeros((4, L), F32)


def window_stats(dst, ones, rb, r1, r2, total_row, scale_row, lo, hi):
    part = slice(16 * lo, 16 * hi)
    v = dst[part]
    w = ones[...]
    hi_part, mid, low = split3(v)
    dot = functools.partial(jnp.dot, preferred_element_type=F32)
    base = dot(hi_part, w)
    rb[part] = base
    r1[part] = base + (dot(mid, w) + dot(low, w))
    q_hi, q_mid, q_low = split3(v * v)
    r2[part] = dot(q_hi, w) + (dot(q_mid, w) + dot(q_low, w))
    dst[part] = hi_part.astype(F32)

    def window_sum(ref, t):
        b = 16 * t
        s = ref[b : b + 4, 0:L] + ref[b + 8 : b + 12, L : 2 * L]
        full = ref[b + 1 : b + 5, 2 * L : 3 * L]
        for r in range(2, 8):
            full = full + ref[b + r : b + r + 4, 2 * L : 3 * L]
        return s + full

    for t in range(lo, hi):
        total_row[4 * t : 4 * t + 4] = window_sum(rb, t)
        mean = window_sum(r1, t) * (1.0 / M)
        power = window_sum(r2, t) * (1.0 / M)
        spread = jnp.maximum(power - mean * mean, 0.0)
        scale_row[4 * t : 4 * t + 4] = lax.rsqrt(spread + 1e-05) * (1.0 / M**0.5)


def turned(rows, base, which, first, g):
    return [
        pltpu.roll(
            jnp.broadcast_to(rows[pl.ds(base + m, 1), :], (16, L)).astype(BF16),
            (first + 16 * g) % L, 1, stride=1, stride_axis=0,
        )
        for m in which
    ]


def own_blocks(rows, t, masks, lhs_even, lhs_odd):
    none = jnp.zeros((16, L), BF16)
    for g in range(8):
        mask = masks[16 * g : 16 * g + 16, :] > 0
        r0, r1, r2, r3, r8, r9, r10, r11 = turned(rows, 16 * t, (0, 1, 2, 3, 8, 9, 10, 11), 0, g)
        pick = lambda u, v: jnp.where(mask, u, v)
        left1, left3 = pick(r1, none), pick(r3, none)
        right7, right9 = pick(none, r8), pick(none, r10)
        for half, even, odd in (
            (0, (pick(r0, r1), right7, left1), (left1, pick(r8, r9), right7)),
            (1, (pick(r2, r3), right9, left3), (left3, pick(r10, r11), right9)),
        ):
            part = slice(L * half + 16 * g, L * half + 16 * g + 16)
            for k in range(3):
                lhs_even[t, part, L * k : L * k + L] = even[k]
                lhs_odd[t, part, L * k : L * k + L] = odd[k]


def shear(rows, base, out, masks):
    for g in range(8):
        mask = masks[16 * g : 16 * g + 16, :] > 0
        turns = turned(rows, base, range(12), 1, g)
        for m in range(11):
            out[16 * g : 16 * g + 16, L * m : L * m + L] = jnp.where(mask, turns[m], turns[m + 1])


def kernel(
    x_ref, out_ref, ones, anti, xmask, ymask, xf, y0, y1, sums, xs, ys0, ys1, rb, r1, r2,
    xtot, xscale, ytot0, yscale0, ytot1, yscale1,
    lhs_even, lhs_odd, fcol, ha0, ha1, hb0, hb1, na0, na1, nb0, nb1, se0, se1, so0, so1, sz0, sz1, racc, col0, col1, got0, got1,
    send_sem, recv_sem, load_sem,
):
    tiles = x_ref.shape[0] // 4
    rows = x_ref.shape[0]
    q = lax.axis_index("qry")
    r = lax.axis_index("ref")
    nq = lax.axis_size("qry")
    nr = lax.axis_size("ref")
    valid = nq * nr * rows * L - M + 1

    def wrap(a, n):
        return lax.rem(a + 2 * n, n)

    def at(flat):
        flat = lax.rem(flat + nq * nr, nq * nr)
        return flat // nr, lax.rem(flat, nr)

    me = q * nr + r
    nextq = wrap(q + 1, nq)
    nextr = wrap(r + 1, nr)
    prevq = wrap(q - 1, nq)
    prevr = wrap(r - 1, nr)
    after = at(me + 1)
    before = at(me - 1)
    behind = at(me - nr + 1)
    ahead = at(me + nr - 1)
    working = q >= 1
    above = q < nq - 1
    tailed = jnp.logical_and(working, me < nq * nr - 1)
    far = me >= nr + 1
    gives = jnp.logical_and(me >= 1, me <= nq * nr - nr)

    barrier = pltpu.get_barrier_semaphore()
    for source, exists in (
        (after, tailed), ((prevq, r), working), ((prevq, prevr), working), (behind, working),
    ):
        @pl.when(exists)
        def _():
            pl.semaphore_signal(barrier, inc=1, device_id=source, device_id_type=MESH)

    load = pltpu.make_async_copy(x_ref, xf.at[pl.ds(0, rows)], load_sem)
    load.start()
    head = x_ref.at[pl.ds(0, 8)]
    plan = [
        (head, xf.at[pl.ds(rows, 8)], before, far, tailed),
        (x_ref, y0.at[pl.ds(0, rows)], (nextq, r), above, working),
        (x_ref, y1.at[pl.ds(0, rows)], (nextq, nextr), above, working),
        (head, y0.at[pl.ds(rows, 8)], ahead, gives, working),
        (col0, got0, (prevq, r), working, above),
        (col1, got1, (prevq, prevr), working, above),
    ]
    copies = [
        pltpu.make_async_remote_copy(
            src_ref=src, dst_ref=dst, send_sem=send_sem.at[n], recv_sem=recv_sem.at[n],
            device_id=device, device_id_type=MESH,
        )
        for n, (src, dst, device, _, _) in enumerate(plan)
    ]
    listeners = sum(jnp.where(p[3], 1, 0) for p in plan[:4])

    @pl.when(listeners > 0)
    def _():
        pl.semaphore_wait(barrier, listeners)

    for c, p in zip(copies[:4], plan):
        pl.when(p[3])(c.start)

    def arrived(n):
        pl.when(plan[n][4])(copies[n].wait_recv)

    i = lax.broadcasted_iota(jnp.int32, (L, L), 0)
    j = lax.broadcasted_iota(jnp.int32, (L, L), 1)
    flag = lambda c: jnp.where(c, 1.0, 0.0).astype(BF16)
    ones[:, 0:L] = flag(i >= j)
    ones[:, L : 2 * L] = flag(i < j)
    ones[:, 2 * L : 3 * L] = jnp.ones((L, L), BF16)
    anti[...] = flag(i + j == L - 1)
    xmask[...] = flag(j >= i)
    ymask[...] = flag(j <= i)
    load.wait()

    @pl.when(working)
    def _():
        compute(
            arrived, (me, r, nq * nr, valid), out_ref, ones, anti, xmask, ymask,
            xf, y0, y1, sums, xs, ys0, ys1, rb, r1, r2,
            xtot, xscale, ytot0, yscale0, ytot1, yscale1,
            lhs_even, lhs_odd, fcol, ha0, ha1, hb0, hb1, na0, na1, nb0, nb1, se0, se1, so0, so1, sz0, sz1, racc, col0, col1,
        )

    @pl.when(jnp.logical_not(working))
    def _():
        out_ref[...] = jnp.full((rows, L), -1.0, F32)

    for n in (4, 5):
        pl.when(plan[n][3])(copies[n].start)
    for n in (4, 5):
        arrived(n)

        @pl.when(above)
        def _():
            out_ref[...] = jnp.maximum(out_ref[...], (got0, got1)[n - 4][...])

    for c, p in zip(copies, plan):
        pl.when(p[3])(c.wait_send)


def compute(
    arrived, place, out_ref, ones, anti, xmask, ymask,
    xf, y0, y1, sums, xs, ys0, ys1, rb, r1, r2,
    xtot, xscale, ytot0, yscale0, ytot1, yscale1,
    lhs_even, lhs_odd, fcol, ha0, ha1, hb0, hb1, na0, na1, nb0, nb1, se0, se1, so0, so1, sz0, sz1, racc, col0, col1,
):
    me, r, count, valid = place
    rows = out_ref.shape[0]
    tiles = rows // 4

    slot = lax.broadcasted_iota(jnp.int32, (8, L), 0)
    lane = lax.broadcasted_iota(jnp.int32, (8, L), 1)
    parts = lambda v: [p.astype(F32) for p in split3(v)]

    def prepare(t, carry):
        own_blocks(xs, t, xmask, lhs_even, lhs_odd)
        for i in range(4):
            mean = jnp.broadcast_to(xtot[pl.ds(4 * t + i, 1), :] * (-1.0 / M), (8, L))
            hi, mid, low = parts(mean)
            window = me * (rows * L) + TILE * t + L * i + lane
            bias = jnp.where(jnp.logical_and(slot == 6, window >= valid), -BIG, 0.0)
            cols = jnp.where(slot < 3, hi, jnp.where(slot < 5, mid, jnp.where(slot < 6, low, bias)))
            cols = jnp.transpose(jnp.concatenate([cols, jnp.zeros((L - 8, L), F32)], axis=0))
            lhs = lhs_odd if i % 2 else lhs_even
            lhs[t, L * (i // 2) : L * (i // 2) + L, 3 * L : 4 * L] = cols.astype(BF16)
            scale = xscale[pl.ds(4 * t + i, 1), :]
            fcol[t, L * i : L * i + L, :] = jnp.transpose(jnp.broadcast_to(scale, (L, L)))
        middle = xs[pl.ds(16 * t + 2, 8), :]
        empty = jnp.zeros((8, L), F32)
        first = jnp.concatenate([middle, empty], axis=0).astype(BF16)
        second = jnp.concatenate([empty, middle], axis=0).astype(BF16)
        none = jnp.zeros((16, L), BF16)
        for k, v in enumerate((first, second, none, none)):
            lhs_even[t, 256:272, L * k : L * k + L] = v
        for k, v in enumerate((none, none, first, none)):
            lhs_even[t, 272:288, L * k : L * k + L] = v
            lhs_odd[t, 256:272, L * k : L * k + L] = v
        return carry

    early = tiles - 2

    def query(lo, hi):
        centre_tiles(xf, xs, sums, lo, hi)
        window_stats(xs, ones, rb, r1, r2, xtot, xscale, lo, hi)
        part = slice(16 * lo, 16 * hi)
        xs[part] = jnp.dot(xs[part].astype(BF16), anti[...], preferred_element_type=F32)
        lax.fori_loop(lo, hi, prepare, 0)

    query(0, early)
    arrived(0)

    @pl.when(me == count - 1)
    def _():
        xf[rows : rows + 8] = jnp.zeros((8, L), F32)

    query(early, tiles)
    for n in range(1, 4):
        arrived(n)
    y1[rows : rows + 8] = jnp.where(r >= 1, y0[0:8], xf[0:8])
    for y, ys, ytot, yscale in ((y0, ys0, ytot0, yscale0), (y1, ys1, ytot1, yscale1)):
        centre_tiles(y, ys, sums, 0, tiles)
        window_stats(ys, ones, rb, r1, r2, ytot, yscale, 0, tiles)

    for ref in (na0, na1, nb0, nb1):
        ref[...] = jnp.zeros((L, TILE), BF16)

    def build(t, h0, h1, n0, n1):
        for ys, ytot, h, n in ((ys0, ytot0, h0, n0), (ys1, ytot1, h1, n1)):
            shear(ys, 16 * t, h, ymask)
            for j in range(4):
                hi, mid, low = parts(jnp.broadcast_to(ytot[pl.ds(4 * t + j, 1), :], (8, L)))
                v = jnp.where(slot == 1, mid, jnp.where(slot == 2, low, jnp.where(slot == 4, mid, hi)))
                v = jnp.where(slot < 6, v, jnp.where(slot == 6, 1.0, 0.0))
                v = jnp.concatenate([v, jnp.zeros((8, L), F32)], axis=0)
                n[0:16, L * j : L * j + L] = v.astype(BF16)

    def products(t, h, n, se, so, sz):
        dot = functools.partial(jnp.dot, preferred_element_type=F32)
        block = lambda k: h[:, L * k : L * k + TILE]
        last = n[...]
        se[...] = dot(lhs_even[t], jnp.concatenate([block(0), block(7), block(1), last], axis=0))
        so[...] = dot(lhs_odd[t], jnp.concatenate([block(0), block(7), block(6), last], axis=0))
        sz[...] = dot(lhs_even[t, 256:272, 0:L], h[:, 5 * L : 6 * L])

    def maxima(t, se, so, sz, yscale, col, first):
        scale = [jnp.broadcast_to(yscale[pl.ds(4 * t + j, 1), :], (8, L)) for j in range(4)]

        def middle(row, m):
            if m < 4:
                v = se[256 + row : 257 + row, L * m : L * m + L]
            elif m == 4:
                v = se[272 + row : 273 + row, 3 * L : 4 * L]
            elif m == 5:
                v = sz[row : row + 1, :]
            elif m == 6:
                v = so[256 + row : 257 + row, 0:L]
            else:
                v = se[264 + row : 265 + row, L * (m - 7) : L * (m - 7) + L]
            return jnp.broadcast_to(v, (8, L))

        best = [None] * 4
        for half in range(2):
            shared = []
            for e in range(-2, 4):
                v = [middle(2 * half + k - 2, k + e) for k in range(2, 8)]
                shared.append((v[0] + v[1]) + (v[2] + v[3]) + (v[4] + v[5]))
            for g in range(16):
                turn = [pltpu.roll(c, 8 * g, 1, stride=1, stride_axis=0) for c in shared]
                mask = lane >= slot + 8 * g
                slid = [jnp.where(mask, turn[e + 1], turn[e]) for e in range(5)]
                for odd, s in ((0, se), (1, so)):
                    part = pl.ds(L * half + 8 * g, 8)
                    place = pl.ds(L * (2 * half + odd) + 8 * g, 8)
                    factor = fcol[t, place, :]
                    row = None if first else racc[place, :]
                    for j in range(4):
                        v = s[part, L * j : L * j + L] + slid[j - odd + 1]
                        a = v * scale[j]
                        row = a if row is None else jnp.maximum(row, a)
                        b = v * factor
                        best[j] = b if best[j] is None else jnp.maximum(best[j], b)
                    racc[place, :] = row
        for j in range(4):
            top = jnp.max(best[j], axis=0, keepdims=True)
            col[pl.ds(4 * t + j, 1), :] = jnp.maximum(top * yscale[pl.ds(4 * t + j, 1), :], -1.0)

    def finish(t):
        for i in range(4):
            top = jnp.max(jnp.transpose(racc[L * i : L * i + L, :]), axis=0, keepdims=True)
            out_ref[pl.ds(4 * t + i, 1), :] = top * xscale[pl.ds(4 * t + i, 1), :]

    def one(t, h0, h1, n0, n1):
        products(t, h0, n0, se0, so0, sz0)
        products(t, h1, n1, se1, so1, sz1)
        maxima(t, se0, so0, sz0, yscale0, col0, True)
        maxima(t, se1, so1, sz1, yscale1, col1, False)
        finish(t)

    build(0, ha0, ha1, na0, na1)

    def pair(u, carry):
        build(2 * u + 1, hb0, hb1, nb0, nb1)
        one(2 * u, ha0, ha1, na0, na1)
        build(lax.rem(2 * u + 2, tiles), ha0, ha1, na0, na1)
        one(2 * u + 1, hb0, hb1, nb0, nb1)
        return carry

    lax.fori_loop(0, tiles // 2, pair, 0)

    cell = lax.broadcasted_iota(jnp.int32, (rows, L), 0) * L
    cell = cell + lax.broadcasted_iota(jnp.int32, (rows, L), 1)
    keep = me * (rows * L) + cell < valid
    out_ref[...] = jnp.where(keep, jnp.maximum(out_ref[...], -1.0), -1.0)


def per_device(series):
    rows = series.shape[0] // L
    tiles = rows // 4
    vm = pltpu.VMEM
    seq = vm((rows + 8, L), F32)
    cut = vm((16 * tiles, L), F32)
    sums = vm((16 * tiles, 3 * L), F32)
    line = vm((rows, L), F32)
    wide = vm((L, 11 * L), BF16)
    slots = vm((L, TILE), BF16)
    out = pl.pallas_call(
        kernel,
        out_shape=jax.ShapeDtypeStruct((rows, L), F32),
        in_specs=[pl.BlockSpec(memory_space=pltpu.HBM)],
        out_specs=pl.BlockSpec(memory_space=vm),
        scratch_shapes=[
            vm((L, 3 * L), BF16), vm((L, L), BF16), vm((L, L), BF16), vm((L, L), BF16),
            seq, seq, seq, seq, cut, cut, cut, sums, sums, sums,
            line, line, line, line, line, line,
            vm((tiles, 288, TILE), BF16), vm((tiles, 272, TILE), BF16), vm((tiles, TILE, L), F32),
            wide, wide, wide, wide, slots, slots, slots, slots,
            vm((288, TILE), F32), vm((288, TILE), F32), vm((272, TILE), F32), vm((272, TILE), F32),
            vm((16, L), F32), vm((16, L), F32), vm((TILE, L), F32),
            line, line, line, line,
            pltpu.SemaphoreType.DMA((6,)), pltpu.SemaphoreType.DMA((6,)),
            pltpu.SemaphoreType.DMA,
        ],
        compiler_params=pltpu.CompilerParams(
            collective_id=0, has_side_effects=True, vmem_limit_bytes=48 * 2**20
        ),
    )(series.reshape(rows, L))
    return out.reshape(-1)


def solution(mesh):
    placed = (P(("qry", "ref")),)
    return jax.shard_map(
        per_device, mesh=mesh, in_specs=placed, out_specs=P(("qry", "ref")), check_vma=False
    )
```

```python
import functools

import jax
import jax.numpy as jnp
from jax import lax
from jax.experimental import pallas as pl
from jax.experimental.pallas import tpu as pltpu
from jax.sharding import PartitionSpec as P

M = 1024
TILE = 512
L = 128
F32 = jnp.float32
BF16 = jnp.bfloat16
MESH = pl.DeviceIdType.MESH
BIG = 1e30
GROUP = 4


def split3(v):
    hi = v.astype(BF16)
    rest = v - hi.astype(F32)
    mid = rest.astype(BF16)
    low = (rest - mid.astype(F32)).astype(BF16)
    return hi, mid, low


def centre_tiles(src, dst, sums, lo, hi):
    a, b = 8 * (lo // 2), 8 * ((4 * hi + 11) // 8)
    sums[a:b] = jnp.broadcast_to(jnp.sum(src[a:b], axis=1, keepdims=True), (b - a, L))
    for t in range(lo, hi):
        c = sums[4 * t + 4 : 4 * t + 5] + sums[4 * t + 5 : 4 * t + 6]
        c = c + (sums[4 * t + 6 : 4 * t + 7] + sums[4 * t + 7 : 4 * t + 8])
        c = c * (1.0 / TILE)
        dst[16 * t : 16 * t + 12] = src[4 * t : 4 * t + 12] - c
        dst[16 * t + 12 : 16 * t + 16] = jnp.zeros((4, L), F32)


def window_stats(dst, ones, rb, r1, r2, total_row, scale_row, lo, hi):
    part = slice(16 * lo, 16 * hi)
    v = dst[part]
    w = ones[...]
    hi_part, mid, low = split3(v)
    dot = functools.partial(jnp.dot, preferred_element_type=F32)
    base = dot(hi_part, w)
    rb[part] = base
    r1[part] = base + (dot(mid, w) + dot(low, w))
    q_hi, q_mid, q_low = split3(v * v)
    r2[part] = dot(q_hi, w) + (dot(q_mid, w) + dot(q_low, w))
    dst[part] = hi_part.astype(F32)

    def window_sum(ref, t):
        b = 16 * t
        s = ref[b : b + 4, 0:L] + ref[b + 8 : b + 12, L : 2 * L]
        full = ref[b + 1 : b + 5, 2 * L : 3 * L]
        for r in range(2, 8):
            full = full + ref[b + r : b + r + 4, 2 * L : 3 * L]
        return s + full

    for t in range(lo, hi):
        total_row[4 * t : 4 * t + 4] = window_sum(rb, t)
        mean = window_sum(r1, t) * (1.0 / M)
        power = window_sum(r2, t) * (1.0 / M)
        spread = jnp.maximum(power - mean * mean, 0.0)
        scale_row[4 * t : 4 * t + 4] = lax.rsqrt(spread + 1e-05) * (1.0 / M**0.5)


def turned(rows, base, which, first, g):
    return [
        pltpu.roll(
            jnp.broadcast_to(rows[pl.ds(base + m, 1), :], (16, L)).astype(BF16),
            (first + 16 * g) % L, 1, stride=1, stride_axis=0,
        )
        for m in which
    ]


def own_blocks(rows, t, masks, lhs_even, lhs_odd):
    none = jnp.zeros((16, L), BF16)
    for g in range(8):
        mask = masks[16 * g : 16 * g + 16, :] > 0
        r0, r1, r2, r3, r8, r9, r10, r11 = turned(rows, 16 * t, (0, 1, 2, 3, 8, 9, 10, 11), 0, g)
        pick = lambda u, v: jnp.where(mask, u, v)
        left1, left3 = pick(r1, none), pick(r3, none)
        right7, right9 = pick(none, r8), pick(none, r10)
        for half, even, odd in (
            (0, (pick(r0, r1), right7, left1), (left1, pick(r8, r9), right7)),
            (1, (pick(r2, r3), right9, left3), (left3, pick(r10, r11), right9)),
        ):
            part = slice(L * half + 16 * g, L * half + 16 * g + 16)
            for k in range(3):
                lhs_even[t, part, L * k : L * k + L] = even[k]
                lhs_odd[t, part, L * k : L * k + L] = odd[k]


def shear(rows, base, out, masks, groups):
    for g in groups:
        mask = masks[16 * g : 16 * g + 16, :] > 0
        turns = turned(rows, base, range(12), 1, g)
        for m in range(11):
            out[16 * g : 16 * g + 16, L * m : L * m + L] = jnp.where(mask, turns[m], turns[m + 1])


def kernel(
    x_ref, out_ref, ones, anti, xmask, ymask, xf, y0, y1, sums, xs, ys0, ys1, rb, r1, r2,
    xtot, xscale, ytot0, yscale0, ytot1, yscale1,
    lhs_even, lhs_odd, fcol, ha0, ha1, hb0, hb1, na0, na1, nb0, nb1, se0, se1, so0, so1, sz0, sz1, racc0, racc1, racc2, racc3, col0, col1, got0, got1,
    send_sem, recv_sem, load_sem,
):
    tiles = x_ref.shape[0] // 4
    rows = x_ref.shape[0]
    q = lax.axis_index("qry")
    r = lax.axis_index("ref")
    nq = lax.axis_size("qry")
    nr = lax.axis_size("ref")
    valid = nq * nr * rows * L - M + 1

    def wrap(a, n):
        return lax.rem(a + 2 * n, n)

    def at(flat):
        flat = lax.rem(flat + nq * nr, nq * nr)
        return flat // nr, lax.rem(flat, nr)

    me = q * nr + r
    nextq = wrap(q + 1, nq)
    nextr = wrap(r + 1, nr)
    prevq = wrap(q - 1, nq)
    prevr = wrap(r - 1, nr)
    after = at(me + 1)
    before = at(me - 1)
    behind = at(me - nr + 1)
    ahead = at(me + nr - 1)
    working = q >= 1
    above = q < nq - 1
    tailed = jnp.logical_and(working, me < nq * nr - 1)
    far = me >= nr + 1
    gives = jnp.logical_and(me >= 1, me <= nq * nr - nr)

    barrier = pltpu.get_barrier_semaphore()
    for source, exists in (
        (after, tailed), ((prevq, r), working), ((prevq, prevr), working), (behind, working),
    ):
        @pl.when(exists)
        def _():
            pl.semaphore_signal(barrier, inc=1, device_id=source, device_id_type=MESH)

    load = pltpu.make_async_copy(x_ref, xf.at[pl.ds(0, rows)], load_sem)
    load.start()
    head = x_ref.at[pl.ds(0, 8)]
    plan = [
        (head, xf.at[pl.ds(rows, 8)], before, far, tailed),
        (x_ref, y0.at[pl.ds(0, rows)], (nextq, r), above, working),
        (x_ref, y1.at[pl.ds(0, rows)], (nextq, nextr), above, working),
        (head, y0.at[pl.ds(rows, 8)], ahead, gives, working),
        (col0, got0, (prevq, r), working, above),
        (col1, got1, (prevq, prevr), working, above),
    ]
    copies = [
        pltpu.make_async_remote_copy(
            src_ref=src, dst_ref=dst, send_sem=send_sem.at[n], recv_sem=recv_sem.at[n],
            device_id=device, device_id_type=MESH,
        )
        for n, (src, dst, device, _, _) in enumerate(plan)
    ]
    listeners = sum(jnp.where(p[3], 1, 0) for p in plan[:4])

    @pl.when(listeners > 0)
    def _():
        pl.semaphore_wait(barrier, listeners)

    for c, p in zip(copies[:4], plan):
        pl.when(p[3])(c.start)

    def arrived(n):
        pl.when(plan[n][4])(copies[n].wait_recv)

    def give(t, several, n):
        part = pl.ds(pl.multiple_of(4 * t, 8), 4 * several)
        src, dst, device = plan[n][:3]
        pltpu.make_async_remote_copy(
            src_ref=src.at[part], dst_ref=dst.at[part], send_sem=send_sem.at[n],
            recv_sem=recv_sem.at[n], device_id=device, device_id_type=MESH,
        ).start()

    i = lax.broadcasted_iota(jnp.int32, (L, L), 0)
    j = lax.broadcasted_iota(jnp.int32, (L, L), 1)
    flag = lambda c: jnp.where(c, 1.0, 0.0).astype(BF16)
    ones[:, 0:L] = flag(i >= j)
    ones[:, L : 2 * L] = flag(i < j)
    ones[:, 2 * L : 3 * L] = jnp.ones((L, L), BF16)
    anti[...] = flag(i + j == L - 1)
    xmask[...] = flag(j >= i)
    ymask[...] = flag(j <= i)
    load.wait()

    @pl.when(working)
    def _():
        compute(
            arrived, give, (me, r, nq * nr, valid), out_ref, ones, anti, xmask, ymask,
            xf, y0, y1, sums, xs, ys0, ys1, rb, r1, r2,
            xtot, xscale, ytot0, yscale0, ytot1, yscale1,
            lhs_even, lhs_odd, fcol, ha0, ha1, hb0, hb1, na0, na1, nb0, nb1, se0, se1, so0, so1, sz0, sz1, racc0, racc1, racc2, racc3, col0, col1,
        )

    @pl.when(jnp.logical_not(working))
    def _():
        out_ref[...] = jnp.full((rows, L), -1.0, F32)

    for n in (4, 5):
        arrived(n)

        @pl.when(above)
        def _():
            out_ref[...] = jnp.maximum(out_ref[...], (got0, got1)[n - 4][...])

    for c, p in zip(copies, plan):
        pl.when(p[3])(c.wait_send)


def compute(
    arrived, give, place, out_ref, ones, anti, xmask, ymask,
    xf, y0, y1, sums, xs, ys0, ys1, rb, r1, r2,
    xtot, xscale, ytot0, yscale0, ytot1, yscale1,
    lhs_even, lhs_odd, fcol, ha0, ha1, hb0, hb1, na0, na1, nb0, nb1, se0, se1, so0, so1, sz0, sz1, racc0, racc1, racc2, racc3, col0, col1,
):
    me, r, count, valid = place
    rows = out_ref.shape[0]
    tiles = rows // 4

    slot = lax.broadcasted_iota(jnp.int32, (8, L), 0)
    lane = lax.broadcasted_iota(jnp.int32, (8, L), 1)
    parts = lambda v: [p.astype(F32) for p in split3(v)]

    def prepare(t, carry):
        own_blocks(xs, t, xmask, lhs_even, lhs_odd)
        for i in range(4):
            mean = jnp.broadcast_to(xtot[pl.ds(4 * t + i, 1), :] * (-1.0 / M), (8, L))
            hi, mid, low = parts(mean)
            window = me * (rows * L) + TILE * t + L * i + lane
            bias = jnp.where(jnp.logical_and(slot == 6, window >= valid), -BIG, 0.0)
            cols = jnp.where(slot < 3, hi, jnp.where(slot < 5, mid, jnp.where(slot < 6, low, bias)))
            cols = jnp.transpose(jnp.concatenate([cols, jnp.zeros((L - 8, L), F32)], axis=0))
            lhs = lhs_odd if i % 2 else lhs_even
            lhs[t, L * (i // 2) : L * (i // 2) + L, 3 * L : 4 * L] = cols.astype(BF16)
            scale = xscale[pl.ds(4 * t + i, 1), :]
            fcol[t, L * i : L * i + L, :] = jnp.transpose(jnp.broadcast_to(scale, (L, L)))
        middle = xs[pl.ds(16 * t + 2, 8), :]
        empty = jnp.zeros((8, L), F32)
        first = jnp.concatenate([middle, empty], axis=0).astype(BF16)
        second = jnp.concatenate([empty, middle], axis=0).astype(BF16)
        none = jnp.zeros((16, L), BF16)
        for k, v in enumerate((first, second, none, none)):
            lhs_even[t, 256:272, L * k : L * k + L] = v
        for k, v in enumerate((none, none, first, none)):
            lhs_even[t, 272:288, L * k : L * k + L] = v
            lhs_odd[t, 256:272, L * k : L * k + L] = v
        return carry

    early = tiles - 2

    def query(lo, hi):
        centre_tiles(xf, xs, sums, lo, hi)
        window_stats(xs, ones, rb, r1, r2, xtot, xscale, lo, hi)
        part = slice(16 * lo, 16 * hi)
        xs[part] = jnp.dot(xs[part].astype(BF16), anti[...], preferred_element_type=F32)
        lax.fori_loop(lo, hi, prepare, 0)

    query(0, early)
    for n in range(1, 4):
        arrived(n)
    y1[rows : rows + 8] = jnp.where(r >= 1, y0[0:8], xf[0:8])
    for y, ys, ytot, yscale in ((y0, ys0, ytot0, yscale0), (y1, ys1, ytot1, yscale1)):
        centre_tiles(y, ys, sums, 0, tiles)
        window_stats(ys, ones, rb, r1, r2, ytot, yscale, 0, tiles)

    for ref in (na0, na1, nb0, nb1):
        ref[...] = jnp.zeros((L, TILE), BF16)

    def build(job, quarter):
        t, ys, ytot, h, n = job
        shear(ys, 16 * t, h, ymask, (2 * quarter, 2 * quarter + 1))
        j = quarter
        hi, mid, low = parts(jnp.broadcast_to(ytot[pl.ds(4 * t + j, 1), :], (8, L)))
        v = jnp.where(slot == 1, mid, jnp.where(slot == 2, low, jnp.where(slot == 4, mid, hi)))
        v = jnp.where(slot < 6, v, jnp.where(slot == 6, 1.0, 0.0))
        v = jnp.concatenate([v, jnp.zeros((8, L), F32)], axis=0)
        n[0:16, L * j : L * j + L] = v.astype(BF16)

    def products(job, odd):
        t, h, n, (se, so, sz) = job
        dot = functools.partial(jnp.dot, preferred_element_type=F32)
        block = lambda k: h[:, L * k : L * k + TILE]
        last = n[...]
        if odd:
            so[...] = dot(lhs_odd[t], jnp.concatenate([block(0), block(7), block(6), last], axis=0))
        else:
            se[...] = dot(lhs_even[t], jnp.concatenate([block(0), block(7), block(1), last], axis=0))
            sz[...] = dot(lhs_even[t, 256:272, 0:L], h[:, 5 * L : 6 * L])

    def middle(sums, row, m):
        se, so, sz = sums
        if m < 4:
            v = se[256 + row : 257 + row, L * m : L * m + L]
        elif m == 4:
            v = se[272 + row : 273 + row, 3 * L : 4 * L]
        elif m == 5:
            v = sz[row : row + 1, :]
        elif m == 6:
            v = so[256 + row : 257 + row, 0:L]
        else:
            v = se[264 + row : 265 + row, L * (m - 7) : L * (m - 7) + L]
        return jnp.broadcast_to(v, (8, L))

    def maxima(job, half, state, groups):
        t, sums, yscale, col, racc, first = job
        if "scale" not in state:
            state["scale"] = [
                jnp.broadcast_to(yscale[pl.ds(4 * t + j, 1), :], (8, L)) for j in range(4)
            ]
            state["best"] = [None] * 4
        scale, best = state["scale"], state["best"]
        if ("shared", half) not in state:
            shared = []
            for e in range(-2, 4):
                v = [middle(sums, 2 * half + k - 2, k + e) for k in range(2, 8)]
                shared.append((v[0] + v[1]) + (v[2] + v[3]) + (v[4] + v[5]))
            state["shared", half] = shared
        shared = state["shared", half]
        for g in groups:
            turn = [pltpu.roll(c, 8 * g, 1, stride=1, stride_axis=0) for c in shared]
            mask = lane >= slot + 8 * g
            slid = [jnp.where(mask, turn[e + 1], turn[e]) for e in range(5)]
            for odd, s in ((0, sums[0]), (1, sums[1])):
                part = pl.ds(L * half + 8 * g, 8)
                place = pl.ds(L * (2 * half + odd) + 8 * g, 8)
                factor = fcol[t, place, :]
                row = None if first else racc[place, :]
                for j in range(4):
                    v = s[part, L * j : L * j + L] + slid[j - odd + 1]
                    a = v * scale[j]
                    row = a if row is None else jnp.maximum(row, a)
                    b = v * factor
                    best[j] = b if best[j] is None else jnp.maximum(best[j], b)
                racc[place, :] = row

    def close(job, state):
        t, _, yscale, col, _, _ = job
        for j in range(4):
            top = jnp.max(state["best"][j], axis=0, keepdims=True)
            col[pl.ds(4 * t + j, 1), :] = jnp.maximum(top * yscale[pl.ds(4 * t + j, 1), :], -1.0)

    def finish(t, racc, i):
        top = jnp.max(jnp.transpose(racc[L * i : L * i + L, :]), axis=0, keepdims=True)
        out_ref[pl.ds(4 * t + i, 1), :] = top * xscale[pl.ds(4 * t + i, 1), :]

    def step(product, top, job, rows_of=None, between=None):
        state = {}
        for quarter in range(4):
            half = quarter // 2
            if quarter % 2 == 0:
                products(product, half)
            maxima(top, half, state, range(8 * (quarter % 2), 8 * (quarter % 2) + 8))
            build(job, quarter)
            if rows_of is not None:
                finish(*rows_of, quarter)
            if quarter == 1 and between is not None:
                between()
        close(top, state)

    matrices = ((ha0, na0), (ha1, na1), (hb0, nb0), (hb1, nb1))
    outputs = ((se0, so0, sz0), (se1, so1, sz1))
    queries = ((ys1, ytot1, yscale1, col1), (ys0, ytot0, yscale0, col0))
    raccs = (racc0, racc1, racc2, racc3)

    def tile_of(t, k):
        return t + k % GROUP if k < 2 * GROUP else lax.rem(t + GROUP + k % GROUP, tiles)

    def matrix_job(t, k):
        ys, ytot = queries[k // GROUP % 2][:2]
        return (tile_of(t, k), ys, ytot, *matrices[k % 4])

    def product_job(t, k):
        return (tile_of(t, k), *matrices[k % 4], outputs[k % 2])

    def maxima_job(t, k):
        which = k // GROUP % 2
        return (tile_of(t, k), outputs[k % 2], *queries[which][2:], raccs[k % GROUP], which == 0)

    racc3[...] = jnp.zeros((TILE, L), F32)
    for quarter in range(4):
        build(matrix_job(0, 0), quarter)
    for odd in range(2):
        products(product_job(0, 0), odd)
    for k in (1, 2):
        for quarter in range(4):
            build(matrix_job(0, k), quarter)

    def group(u, carry):
        t = GROUP * u
        pl.when(u > 0)(lambda: give(t - 2, 2, 4))

        @pl.when(u == tiles // GROUP - 1)
        def _():
            arrived(0)

            @pl.when(me == count - 1)
            def _():
                xf[rows : rows + 8] = jnp.zeros((8, L), F32)

            query(early, tiles)

        for k in range(2 * GROUP):
            done = None
            if k == 0:
                done = (lax.rem(t + tiles - 1, tiles), raccs[GROUP - 1])
            elif k > GROUP:
                done = (t + k - GROUP - 1, raccs[k - GROUP - 1])
            between = None
            if k == GROUP:
                between = lambda: give(t, GROUP, 5)
            elif k == GROUP + 2:
                between = lambda: give(t, 2, 4)
            step(product_job(t, k + 1), maxima_job(t, k), matrix_job(t, k + 3), done, between)
        return carry

    lax.fori_loop(0, tiles // GROUP, group, 0)
    give(tiles - 2, 2, 4)
    for i in range(4):
        finish(tiles - 1, racc3, i)
    cell = lax.broadcasted_iota(jnp.int32, (rows, L), 0) * L
    cell = cell + lax.broadcasted_iota(jnp.int32, (rows, L), 1)
    keep = me * (rows * L) + cell < valid
    out_ref[...] = jnp.where(keep, jnp.maximum(out_ref[...], -1.0), -1.0)


def per_device(series):
    rows = series.shape[0] // L
    tiles = rows // 4
    vm = pltpu.VMEM
    seq = vm((rows + 8, L), F32)
    cut = vm((16 * tiles, L), F32)
    sums = vm((16 * tiles, 3 * L), F32)
    line = vm((rows, L), F32)
    wide = vm((L, 11 * L), BF16)
    slots = vm((L, TILE), BF16)
    out = pl.pallas_call(
        kernel,
        out_shape=jax.ShapeDtypeStruct((rows, L), F32),
        in_specs=[pl.BlockSpec(memory_space=pltpu.HBM)],
        out_specs=pl.BlockSpec(memory_space=vm),
        scratch_shapes=[
            vm((L, 3 * L), BF16), vm((L, L), BF16), vm((L, L), BF16), vm((L, L), BF16),
            seq, seq, seq, seq, cut, cut, cut, sums, sums, sums,
            line, line, line, line, line, line,
            vm((tiles, 288, TILE), BF16), vm((tiles, 272, TILE), BF16), vm((tiles, TILE, L), F32),
            wide, wide, wide, wide, slots, slots, slots, slots,
            vm((288, TILE), F32), vm((288, TILE), F32), vm((272, TILE), F32), vm((272, TILE), F32),
            vm((16, L), F32), vm((16, L), F32), vm((TILE, L), F32), vm((TILE, L), F32),
            vm((TILE, L), F32), vm((TILE, L), F32),
            line, line, line, line,
            pltpu.SemaphoreType.DMA((6,)), pltpu.SemaphoreType.DMA((6,)),
            pltpu.SemaphoreType.DMA,
        ],
        compiler_params=pltpu.CompilerParams(
            collective_id=0, has_side_effects=True, vmem_limit_bytes=48 * 2**20
        ),
    )(pltpu.with_memory_space_constraint(series.reshape(rows, L), pltpu.HBM))
    return out.reshape(-1)


def solution(mesh):
    placed = (P(("qry", "ref")),)
    return jax.shard_map(
        per_device, mesh=mesh, in_specs=placed, out_specs=P(("qry", "ref")), check_vma=False
    )
```

```python
import functools

import jax
import jax.numpy as jnp
from jax import lax
from jax.experimental import pallas as pl
from jax.experimental.pallas import tpu as pltpu
from jax.sharding import PartitionSpec as P

M = 1024
TILE = 512
L = 128
F32 = jnp.float32
BF16 = jnp.bfloat16
MESH = pl.DeviceIdType.MESH
BIG = 1e30
GROUP = 4


def split3(v):
    hi = v.astype(BF16)
    rest = v - hi.astype(F32)
    mid = rest.astype(BF16)
    low = (rest - mid.astype(F32)).astype(BF16)
    return hi, mid, low


def centre_tiles(src, dst, sums, lo, hi):
    a, b = 8 * (lo // 2), 8 * ((4 * hi + 11) // 8)
    sums[a:b] = jnp.broadcast_to(jnp.sum(src[a:b], axis=1, keepdims=True), (b - a, L))
    for t in range(lo, hi):
        c = sums[4 * t + 4 : 4 * t + 5] + sums[4 * t + 5 : 4 * t + 6]
        c = c + (sums[4 * t + 6 : 4 * t + 7] + sums[4 * t + 7 : 4 * t + 8])
        c = c * (1.0 / TILE)
        dst[16 * t : 16 * t + 12] = src[4 * t : 4 * t + 12] - c
        dst[16 * t + 12 : 16 * t + 16] = jnp.zeros((4, L), F32)


def window_stats(dst, ones, rb, r1, r2, total_row, scale_row, lo, hi):
    part = slice(16 * lo, 16 * hi)
    v = dst[part]
    w = ones[...]
    hi_part, mid, low = split3(v)
    dot = functools.partial(jnp.dot, preferred_element_type=F32)
    base = dot(hi_part, w)
    rb[part] = base
    r1[part] = base + (dot(mid, w) + dot(low, w))
    q_hi, q_mid, q_low = split3(v * v)
    r2[part] = dot(q_hi, w) + (dot(q_mid, w) + dot(q_low, w))
    dst[part] = hi_part.astype(F32)

    def window_sum(ref, t):
        b = 16 * t
        s = ref[b : b + 4, 0:L] + ref[b + 8 : b + 12, L : 2 * L]
        full = ref[b + 1 : b + 5, 2 * L : 3 * L]
        for r in range(2, 8):
            full = full + ref[b + r : b + r + 4, 2 * L : 3 * L]
        return s + full

    for t in range(lo, hi):
        total_row[4 * t : 4 * t + 4] = window_sum(rb, t)
        mean = window_sum(r1, t) * (1.0 / M)
        power = window_sum(r2, t) * (1.0 / M)
        spread = jnp.maximum(power - mean * mean, 0.0)
        scale_row[4 * t : 4 * t + 4] = lax.rsqrt(spread + 1e-05) * (1.0 / M**0.5)


def turned(rows, base, which, first, g):
    return [
        pltpu.roll(
            jnp.broadcast_to(rows[pl.ds(base + m, 1), :], (16, L)).astype(BF16),
            (first + 16 * g) % L, 1, stride=1, stride_axis=0,
        )
        for m in which
    ]


def own_blocks(rows, t, masks, lhs_even, lhs_odd):
    none = jnp.zeros((16, L), BF16)
    for g in range(8):
        mask = masks[16 * g : 16 * g + 16, :] > 0
        r0, r1, r2, r3, r8, r9, r10, r11 = turned(rows, 16 * t, (0, 1, 2, 3, 8, 9, 10, 11), 0, g)
        pick = lambda u, v: jnp.where(mask, u, v)
        left1, left3 = pick(r1, none), pick(r3, none)
        right7, right9 = pick(none, r8), pick(none, r10)
        for half, even, odd in (
            (0, (pick(r0, r1), right7, left1), (left1, pick(r8, r9), right7)),
            (1, (pick(r2, r3), right9, left3), (left3, pick(r10, r11), right9)),
        ):
            part = slice(L * half + 16 * g, L * half + 16 * g + 16)
            for k in range(3):
                lhs_even[t, part, L * k : L * k + L] = even[k]
                lhs_odd[t, part, L * k : L * k + L] = odd[k]


def shear(rows, base, out, masks, groups):
    for g in groups:
        mask = masks[16 * g : 16 * g + 16, :] > 0
        turns = turned(rows, base, range(12), 1, g)
        for m in range(11):
            out[16 * g : 16 * g + 16, L * m : L * m + L] = jnp.where(mask, turns[m], turns[m + 1])


def kernel(
    x_ref, out_ref, ones, anti, xmask, ymask, xf, y0, y1, sums, xs, ys0, ys1, rb, r1, r2,
    xtot, xscale, ytot0, yscale0, ytot1, yscale1,
    lhs_even, lhs_odd, fcol, ha0, ha1, hb0, hb1, na0, na1, nb0, nb1, se0, se1, so0, so1, sz0, sz1, racc0, racc1, racc2, racc3, col0, col1, got0, got1,
    send_sem, recv_sem, load_sem,
):
    tiles = x_ref.shape[0] // 4
    rows = x_ref.shape[0]
    q = lax.axis_index("qry")
    r = lax.axis_index("ref")
    nq = lax.axis_size("qry")
    nr = lax.axis_size("ref")
    valid = nq * nr * rows * L - M + 1

    def wrap(a, n):
        return lax.rem(a + 2 * n, n)

    def at(flat):
        flat = lax.rem(flat + nq * nr, nq * nr)
        return flat // nr, lax.rem(flat, nr)

    me = q * nr + r
    nextq = wrap(q + 1, nq)
    nextr = wrap(r + 1, nr)
    prevq = wrap(q - 1, nq)
    prevr = wrap(r - 1, nr)
    after = at(me + 1)
    before = at(me - 1)
    behind = at(me - nr + 1)
    ahead = at(me + nr - 1)
    working = q >= 1
    above = q < nq - 1
    tailed = jnp.logical_and(working, me < nq * nr - 1)
    far = me >= nr + 1
    gives = jnp.logical_and(me >= 1, me <= nq * nr - nr)

    barrier = pltpu.get_barrier_semaphore()
    for source, exists in (
        (after, tailed), ((prevq, r), working), ((prevq, prevr), working), (behind, working),
    ):
        @pl.when(exists)
        def _():
            pl.semaphore_signal(barrier, inc=1, device_id=source, device_id_type=MESH)

    load = pltpu.make_async_copy(x_ref, xf.at[pl.ds(0, rows)], load_sem)
    load.start()
    head = x_ref.at[pl.ds(0, 8)]
    plan = [
        (head, xf.at[pl.ds(rows, 8)], before, far, tailed),
        (x_ref, y0.at[pl.ds(0, rows)], (nextq, r), above, working),
        (x_ref, y1.at[pl.ds(0, rows)], (nextq, nextr), above, working),
        (head, y0.at[pl.ds(rows, 8)], ahead, gives, working),
        (col0, got0, (prevq, r), working, above),
        (col1, got1, (prevq, prevr), working, above),
    ]
    copies = [
        pltpu.make_async_remote_copy(
            src_ref=src, dst_ref=dst, send_sem=send_sem.at[n], recv_sem=recv_sem.at[n],
            device_id=device, device_id_type=MESH,
        )
        for n, (src, dst, device, _, _) in enumerate(plan)
    ]
    listeners = sum(jnp.where(p[3], 1, 0) for p in plan[:4])

    @pl.when(listeners > 0)
    def _():
        pl.semaphore_wait(barrier, listeners)

    for n in (2, 1, 3, 0):
        pl.when(plan[n][3])(copies[n].start)

    def arrived(n):
        pl.when(plan[n][4])(copies[n].wait_recv)

    def give(t, several, n):
        part = pl.ds(pl.multiple_of(4 * t, 8), 4 * several)
        src, dst, device = plan[n][:3]
        pltpu.make_async_remote_copy(
            src_ref=src.at[part], dst_ref=dst.at[part], send_sem=send_sem.at[n],
            recv_sem=recv_sem.at[n], device_id=device, device_id_type=MESH,
        ).start()

    i = lax.broadcasted_iota(jnp.int32, (L, L), 0)
    j = lax.broadcasted_iota(jnp.int32, (L, L), 1)
    flag = lambda c: jnp.where(c, 1.0, 0.0).astype(BF16)
    ones[:, 0:L] = flag(i >= j)
    ones[:, L : 2 * L] = flag(i < j)
    ones[:, 2 * L : 3 * L] = jnp.ones((L, L), BF16)
    anti[...] = flag(i + j == L - 1)
    xmask[...] = flag(j >= i)
    ymask[...] = flag(j <= i)
    load.wait()

    @pl.when(working)
    def _():
        compute(
            arrived, give, (me, r, nq * nr, valid), out_ref, ones, anti, xmask, ymask,
            xf, y0, y1, sums, xs, ys0, ys1, rb, r1, r2,
            xtot, xscale, ytot0, yscale0, ytot1, yscale1,
            lhs_even, lhs_odd, fcol, ha0, ha1, hb0, hb1, na0, na1, nb0, nb1, se0, se1, so0, so1, sz0, sz1, racc0, racc1, racc2, racc3, col0, col1,
        )

    @pl.when(jnp.logical_not(working))
    def _():
        out_ref[...] = jnp.full((rows, L), -1.0, F32)

    for n in (4, 5):
        arrived(n)

        @pl.when(above)
        def _():
            out_ref[...] = jnp.maximum(out_ref[...], (got0, got1)[n - 4][...])

    for c, p in zip(copies, plan):
        pl.when(p[3])(c.wait_send)


def compute(
    arrived, give, place, out_ref, ones, anti, xmask, ymask,
    xf, y0, y1, sums, xs, ys0, ys1, rb, r1, r2,
    xtot, xscale, ytot0, yscale0, ytot1, yscale1,
    lhs_even, lhs_odd, fcol, ha0, ha1, hb0, hb1, na0, na1, nb0, nb1, se0, se1, so0, so1, sz0, sz1, racc0, racc1, racc2, racc3, col0, col1,
):
    me, r, count, valid = place
    rows = out_ref.shape[0]
    tiles = rows // 4

    slot = lax.broadcasted_iota(jnp.int32, (8, L), 0)
    lane = lax.broadcasted_iota(jnp.int32, (8, L), 1)
    parts = lambda v: [p.astype(F32) for p in split3(v)]

    def prepare(t, carry):
        own_blocks(xs, t, xmask, lhs_even, lhs_odd)
        for i in range(4):
            mean = jnp.broadcast_to(xtot[pl.ds(4 * t + i, 1), :] * (-1.0 / M), (8, L))
            hi, mid, low = parts(mean)
            window = me * (rows * L) + TILE * t + L * i + lane
            bias = jnp.where(jnp.logical_and(slot == 6, window >= valid), -BIG, 0.0)
            cols = jnp.where(slot < 3, hi, jnp.where(slot < 5, mid, jnp.where(slot < 6, low, bias)))
            cols = jnp.transpose(jnp.concatenate([cols, jnp.zeros((L - 8, L), F32)], axis=0))
            lhs = lhs_odd if i % 2 else lhs_even
            lhs[t, L * (i // 2) : L * (i // 2) + L, 3 * L : 4 * L] = cols.astype(BF16)
            scale = xscale[pl.ds(4 * t + i, 1), :]
            fcol[t, L * i : L * i + L, :] = jnp.transpose(jnp.broadcast_to(scale, (L, L)))
        middle = xs[pl.ds(16 * t + 2, 8), :]
        empty = jnp.zeros((8, L), F32)
        first = jnp.concatenate([middle, empty], axis=0).astype(BF16)
        second = jnp.concatenate([empty, middle], axis=0).astype(BF16)
        none = jnp.zeros((16, L), BF16)
        for k, v in enumerate((first, second, none, none)):
            lhs_even[t, 256:272, L * k : L * k + L] = v
        for k, v in enumerate((none, none, first, none)):
            lhs_even[t, 272:288, L * k : L * k + L] = v
            lhs_odd[t, 256:272, L * k : L * k + L] = v
        return carry

    early = tiles - 2

    def query(lo, hi):
        centre_tiles(xf, xs, sums, lo, hi)
        window_stats(xs, ones, rb, r1, r2, xtot, xscale, lo, hi)
        part = slice(16 * lo, 16 * hi)
        xs[part] = jnp.dot(xs[part].astype(BF16), anti[...], preferred_element_type=F32)
        lax.fori_loop(lo, hi, prepare, 0)

    query(0, early)
    for n in range(1, 4):
        arrived(n)
    y1[rows : rows + 8] = jnp.where(r >= 1, y0[0:8], xf[0:8])
    for y, ys, ytot, yscale in ((y0, ys0, ytot0, yscale0), (y1, ys1, ytot1, yscale1)):
        centre_tiles(y, ys, sums, 0, tiles)
        window_stats(ys, ones, rb, r1, r2, ytot, yscale, 0, tiles)

    for ref in (na0, na1, nb0, nb1):
        ref[...] = jnp.zeros((L, TILE), BF16)

    def build(job, quarter):
        t, ys, ytot, h, n = job
        shear(ys, 16 * t, h, ymask, (2 * quarter, 2 * quarter + 1))
        j = quarter
        hi, mid, low = parts(jnp.broadcast_to(ytot[pl.ds(4 * t + j, 1), :], (8, L)))
        v = jnp.where(slot == 1, mid, jnp.where(slot == 2, low, jnp.where(slot == 4, mid, hi)))
        v = jnp.where(slot < 6, v, jnp.where(slot == 6, 1.0, 0.0))
        v = jnp.concatenate([v, jnp.zeros((8, L), F32)], axis=0)
        n[0:16, L * j : L * j + L] = v.astype(BF16)

    def products(job, odd):
        t, h, n, (se, so, sz) = job
        dot = functools.partial(jnp.dot, preferred_element_type=F32)
        block = lambda k: h[:, L * k : L * k + TILE]
        last = n[...]
        if odd:
            so[...] = dot(lhs_odd[t], jnp.concatenate([block(0), block(7), block(6), last], axis=0))
        else:
            se[...] = dot(lhs_even[t], jnp.concatenate([block(0), block(7), block(1), last], axis=0))
            sz[...] = dot(lhs_even[t, 256:272, 0:L], h[:, 5 * L : 6 * L])

    def middle(sums, row, m):
        se, so, sz = sums
        if m < 4:
            v = se[256 + row : 257 + row, L * m : L * m + L]
        elif m == 4:
            v = se[272 + row : 273 + row, 3 * L : 4 * L]
        elif m == 5:
            v = sz[row : row + 1, :]
        elif m == 6:
            v = so[256 + row : 257 + row, 0:L]
        else:
            v = se[264 + row : 265 + row, L * (m - 7) : L * (m - 7) + L]
        return jnp.broadcast_to(v, (8, L))

    def maxima(job, half, state, groups):
        t, sums, yscale, col, racc, first = job
        if "scale" not in state:
            state["scale"] = [
                jnp.broadcast_to(yscale[pl.ds(4 * t + j, 1), :], (8, L)) for j in range(4)
            ]
            state["best"] = [None] * 4
        scale, best = state["scale"], state["best"]
        if ("shared", half) not in state:
            shared = []
            for e in range(-2, 4):
                v = [middle(sums, 2 * half + k - 2, k + e) for k in range(2, 8)]
                shared.append((v[0] + v[1]) + (v[2] + v[3]) + (v[4] + v[5]))
            state["shared", half] = shared
        shared = state["shared", half]
        for g in groups:
            turn = [pltpu.roll(c, 8 * g, 1, stride=1, stride_axis=0) for c in shared]
            mask = lane >= slot + 8 * g
            slid = [jnp.where(mask, turn[e + 1], turn[e]) for e in range(5)]
            for odd, s in ((0, sums[0]), (1, sums[1])):
                part = pl.ds(L * half + 8 * g, 8)
                place = pl.ds(L * (2 * half + odd) + 8 * g, 8)
                factor = fcol[t, place, :]
                row = None if first else racc[place, :]
                for j in range(4):
                    v = s[part, L * j : L * j + L] + slid[j - odd + 1]
                    a = v * scale[j]
                    row = a if row is None else jnp.maximum(row, a)
                    b = v * factor
                    best[j] = b if best[j] is None else jnp.maximum(best[j], b)
                racc[place, :] = row

    def close(job, state):
        t, _, yscale, col, _, _ = job
        for j in range(4):
            top = jnp.max(state["best"][j], axis=0, keepdims=True)
            col[pl.ds(4 * t + j, 1), :] = jnp.maximum(top * yscale[pl.ds(4 * t + j, 1), :], -1.0)

    def finish(t, racc, i):
        top = jnp.max(jnp.transpose(racc[L * i : L * i + L, :]), axis=0, keepdims=True)
        out_ref[pl.ds(4 * t + i, 1), :] = top * xscale[pl.ds(4 * t + i, 1), :]

    def step(product, top, job, rows_of=None, between=None):
        state = {}
        for quarter in range(4):
            half = quarter // 2
            if quarter % 2 == 0 and product is not None:
                products(product, half)
            maxima(top, half, state, range(8 * (quarter % 2), 8 * (quarter % 2) + 8))
            if job is not None:
                build(job, quarter)
            if rows_of is not None:
                finish(*rows_of, quarter)
            if quarter == 1 and between is not None:
                between()
        close(top, state)

    matrices = ((ha0, na0), (ha1, na1), (hb0, nb0), (hb1, nb1))
    outputs = ((se0, so0, sz0), (se1, so1, sz1))
    queries = ((ys1, ytot1, yscale1, col1), (ys0, ytot0, yscale0, col0))
    raccs = (racc0, racc1, racc2, racc3)

    def tile_of(t, k):
        return t + k % GROUP if k < 2 * GROUP else lax.rem(t + GROUP + k % GROUP, tiles)

    def matrix_job(t, k):
        ys, ytot = queries[k // GROUP % 2][:2]
        return (tile_of(t, k), ys, ytot, *matrices[k % 4])

    def product_job(t, k):
        return (tile_of(t, k), *matrices[k % 4], outputs[k % 2])

    def maxima_job(t, k):
        which = k // GROUP % 2
        return (tile_of(t, k), outputs[k % 2], *queries[which][2:], raccs[k % GROUP], which == 0)

    racc3[...] = jnp.zeros((TILE, L), F32)
    for quarter in range(4):
        build(matrix_job(0, 0), quarter)
    for odd in range(2):
        products(product_job(0, 0), odd)
    for k in (1, 2):
        for quarter in range(4):
            build(matrix_job(0, k), quarter)

    def group(t, final):
        for k in range(2 * GROUP):
            done = None
            if k == 0:
                done = (lax.rem(t + tiles - 1, tiles), raccs[GROUP - 1])
            elif k > GROUP:
                done = (t + k - GROUP - 1, raccs[k - GROUP - 1])
            between = None
            if k == GROUP:
                between = lambda: give(t, GROUP, 5)
            elif k == GROUP + 2:
                between = lambda: give(t, 2, 4)
            following = None if final and k + 1 >= 2 * GROUP else product_job(t, k + 1)
            later = None if final and k + 3 >= 2 * GROUP else matrix_job(t, k + 3)
            step(following, maxima_job(t, k), later, done, between)

    def groups(u, carry):
        pl.when(u > 0)(lambda: give(GROUP * u - 2, 2, 4))
        group(GROUP * u, False)
        return carry

    lax.fori_loop(0, tiles // GROUP - 1, groups, 0)
    give(tiles - GROUP - 2, 2, 4)
    arrived(0)

    @pl.when(me == count - 1)
    def _():
        xf[rows : rows + 8] = jnp.zeros((8, L), F32)

    query(early, tiles)
    group(tiles - GROUP, True)
    give(tiles - 2, 2, 4)
    for i in range(4):
        finish(tiles - 1, racc3, i)
    cell = lax.broadcasted_iota(jnp.int32, (rows, L), 0) * L
    cell = cell + lax.broadcasted_iota(jnp.int32, (rows, L), 1)
    keep = me * (rows * L) + cell < valid
    out_ref[...] = jnp.where(keep, jnp.maximum(out_ref[...], -1.0), -1.0)


def per_device(series):
    rows = series.shape[0] // L
    tiles = rows // 4
    vm = pltpu.VMEM
    seq = vm((rows + 8, L), F32)
    cut = vm((16 * tiles, L), F32)
    sums = vm((16 * tiles, 3 * L), F32)
    line = vm((rows, L), F32)
    wide = vm((L, 11 * L), BF16)
    slots = vm((L, TILE), BF16)
    out = pl.pallas_call(
        kernel,
        out_shape=jax.ShapeDtypeStruct((rows, L), F32),
        in_specs=[pl.BlockSpec(memory_space=pltpu.HBM)],
        out_specs=pl.BlockSpec(memory_space=vm),
        scratch_shapes=[
            vm((L, 3 * L), BF16), vm((L, L), BF16), vm((L, L), BF16), vm((L, L), BF16),
            seq, seq, seq, seq, cut, cut, cut, sums, sums, sums,
            line, line, line, line, line, line,
            vm((tiles, 288, TILE), BF16), vm((tiles, 272, TILE), BF16), vm((tiles, TILE, L), F32),
            wide, wide, wide, wide, slots, slots, slots, slots,
            vm((288, TILE), F32), vm((288, TILE), F32), vm((272, TILE), F32), vm((272, TILE), F32),
            vm((16, L), F32), vm((16, L), F32), vm((TILE, L), F32), vm((TILE, L), F32),
            vm((TILE, L), F32), vm((TILE, L), F32),
            line, line, line, line,
            pltpu.SemaphoreType.DMA((6,)), pltpu.SemaphoreType.DMA((6,)),
            pltpu.SemaphoreType.DMA,
        ],
        compiler_params=pltpu.CompilerParams(
            collective_id=0, has_side_effects=True, vmem_limit_bytes=48 * 2**20
        ),
    )(pltpu.with_memory_space_constraint(series.reshape(rows, L), pltpu.HBM))
    return out.reshape(-1)


def solution(mesh):
    placed = (P(("qry", "ref")),)
    return jax.shard_map(
        per_device, mesh=mesh, in_specs=placed, out_specs=P(("qry", "ref")), check_vma=False
    )
```

```python
import functools

import jax
import jax.numpy as jnp
from jax import lax
from jax.experimental import pallas as pl
from jax.experimental.pallas import tpu as pltpu
from jax.sharding import PartitionSpec as P

M = 1024
TILE = 512
L = 128
F32 = jnp.float32
BF16 = jnp.bfloat16
MESH = pl.DeviceIdType.MESH
BIG = 1e30
GROUP = 4


def split3(v):
    hi = v.astype(BF16)
    rest = v - hi.astype(F32)
    mid = rest.astype(BF16)
    low = (rest - mid.astype(F32)).astype(BF16)
    return hi, mid, low


def centre_tiles(src, dst, sums, lo, hi):
    a, b = 8 * (lo // 2), 8 * ((4 * hi + 11) // 8)
    sums[a:b] = jnp.broadcast_to(jnp.sum(src[a:b], axis=1, keepdims=True), (b - a, L))
    for t in range(lo, hi):
        c = sums[4 * t + 4 : 4 * t + 5] + sums[4 * t + 5 : 4 * t + 6]
        c = c + (sums[4 * t + 6 : 4 * t + 7] + sums[4 * t + 7 : 4 * t + 8])
        c = c * (1.0 / TILE)
        dst[16 * t : 16 * t + 12] = src[4 * t : 4 * t + 12] - c
        dst[16 * t + 12 : 16 * t + 16] = jnp.zeros((4, L), F32)


def window_stats(dst, ones, rb, r1, r2, total_row, scale_row, lo, hi):
    part = slice(16 * lo, 16 * hi)
    v = dst[part]
    w = ones[...]
    hi_part, mid, low = split3(v)
    dot = functools.partial(jnp.dot, preferred_element_type=F32)
    base = dot(hi_part, w)
    rb[part] = base
    r1[part] = base + (dot(mid, w) + dot(low, w))
    q_hi, q_mid, q_low = split3(v * v)
    r2[part] = dot(q_hi, w) + (dot(q_mid, w) + dot(q_low, w))
    dst[part] = hi_part.astype(F32)

    def window_sum(ref, t):
        b = 16 * t
        s = ref[b : b + 4, 0:L] + ref[b + 8 : b + 12, L : 2 * L]
        full = ref[b + 1 : b + 5, 2 * L : 3 * L]
        for r in range(2, 8):
            full = full + ref[b + r : b + r + 4, 2 * L : 3 * L]
        return s + full

    for t in range(lo, hi):
        total_row[4 * t : 4 * t + 4] = window_sum(rb, t)
        mean = window_sum(r1, t) * (1.0 / M)
        power = window_sum(r2, t) * (1.0 / M)
        spread = jnp.maximum(power - mean * mean, 0.0)
        scale_row[4 * t : 4 * t + 4] = lax.rsqrt(spread + 1e-05) * (1.0 / M**0.5)


def turned(rows, base, which, first, g):
    return [
        pltpu.roll(
            jnp.broadcast_to(rows[pl.ds(base + m, 1), :], (16, L)).astype(BF16),
            (first + 16 * g) % L, 1, stride=1, stride_axis=0,
        )
        for m in which
    ]


def own_blocks(rows, t, masks, lhs_even, lhs_odd):
    none = jnp.zeros((16, L), BF16)
    for g in range(8):
        mask = masks[16 * g : 16 * g + 16, :] > 0
        r0, r1, r2, r3, r8, r9, r10, r11 = turned(rows, 16 * t, (0, 1, 2, 3, 8, 9, 10, 11), 0, g)
        pick = lambda u, v: jnp.where(mask, u, v)
        left1, left3 = pick(r1, none), pick(r3, none)
        right7, right9 = pick(none, r8), pick(none, r10)
        for half, even, odd in (
            (0, (pick(r0, r1), right7, left1), (left1, pick(r8, r9), right7)),
            (1, (pick(r2, r3), right9, left3), (left3, pick(r10, r11), right9)),
        ):
            part = slice(L * half + 16 * g, L * half + 16 * g + 16)
            for k in range(3):
                lhs_even[t, part, L * k : L * k + L] = even[k]
                lhs_odd[t, part, L * k : L * k + L] = odd[k]


def shear(rows, base, out, masks, groups):
    for g in groups:
        mask = masks[16 * g : 16 * g + 16, :] > 0
        turns = turned(rows, base, range(12), 1, g)
        for m in range(11):
            out[16 * g : 16 * g + 16, L * m : L * m + L] = jnp.where(mask, turns[m], turns[m + 1])


def kernel(
    x_ref, out_ref, ones, anti, xmask, ymask, xf, y0, y1, sums, xs, ys0, ys1, rb, r1, r2,
    xtot, xscale, ytot0, yscale0, ytot1, yscale1,
    lhs_even, lhs_odd, fcol, ha0, ha1, hb0, hb1, na0, na1, nb0, nb1, se0, se1, so0, so1, sz0, sz1, racc0, racc1, racc2, racc3, col0, col1, got0, got1,
    send_sem, recv_sem, load_sem,
):
    tiles = x_ref.shape[0] // 4
    rows = x_ref.shape[0]
    q = lax.axis_index("qry")
    r = lax.axis_index("ref")
    nq = lax.axis_size("qry")
    nr = lax.axis_size("ref")
    valid = nq * nr * rows * L - M + 1

    def wrap(a, n):
        return lax.rem(a + 2 * n, n)

    def at(flat):
        flat = lax.rem(flat + nq * nr, nq * nr)
        return flat // nr, lax.rem(flat, nr)

    me = q * nr + r
    nextq = wrap(q + 1, nq)
    nextr = wrap(r + 1, nr)
    prevq = wrap(q - 1, nq)
    prevr = wrap(r - 1, nr)
    after = at(me + 1)
    before = at(me - 1)
    behind = at(me - nr + 1)
    ahead = at(me + nr - 1)
    working = q >= 1
    above = q < nq - 1
    tailed = jnp.logical_and(working, me < nq * nr - 1)
    far = me >= nr + 1
    gives = jnp.logical_and(me >= 1, me <= nq * nr - nr)

    barrier = pltpu.get_barrier_semaphore()
    for source, exists in (
        (after, tailed), ((prevq, r), working), ((prevq, prevr), working), (behind, working),
    ):
        @pl.when(exists)
        def _():
            pl.semaphore_signal(barrier, inc=1, device_id=source, device_id_type=MESH)

    load = pltpu.make_async_copy(x_ref, xf.at[pl.ds(0, rows)], load_sem)
    load.start()
    head = x_ref.at[pl.ds(0, 8)]
    plan = [
        (head, xf.at[pl.ds(rows, 8)], before, far, tailed),
        (x_ref, y0.at[pl.ds(0, rows)], (nextq, r), above, working),
        (x_ref, y1.at[pl.ds(0, rows)], (nextq, nextr), above, working),
        (head, y0.at[pl.ds(rows, 8)], ahead, gives, working),
        (col0, got0, (prevq, r), working, above),
        (col1, got1, (prevq, prevr), working, above),
    ]
    copies = [
        pltpu.make_async_remote_copy(
            src_ref=src, dst_ref=dst, send_sem=send_sem.at[n], recv_sem=recv_sem.at[n],
            device_id=device, device_id_type=MESH,
        )
        for n, (src, dst, device, _, _) in enumerate(plan)
    ]
    listeners = sum(jnp.where(p[3], 1, 0) for p in plan[:4])

    @pl.when(listeners > 0)
    def _():
        pl.semaphore_wait(barrier, listeners)

    for n in (2, 1, 3, 0):
        pl.when(plan[n][3])(copies[n].start)

    def arrived(n):
        pl.when(plan[n][4])(copies[n].wait_recv)

    def give(t, several, n):
        part = pl.ds(pl.multiple_of(4 * t, 8), 4 * several)
        src, dst, device = plan[n][:3]
        pltpu.make_async_remote_copy(
            src_ref=src.at[part], dst_ref=dst.at[part], send_sem=send_sem.at[n],
            recv_sem=recv_sem.at[n], device_id=device, device_id_type=MESH,
        ).start()

    i = lax.broadcasted_iota(jnp.int32, (L, L), 0)
    j = lax.broadcasted_iota(jnp.int32, (L, L), 1)
    flag = lambda c: jnp.where(c, 1.0, 0.0).astype(BF16)
    ones[:, 0:L] = flag(i >= j)
    ones[:, L : 2 * L] = flag(i < j)
    ones[:, 2 * L : 3 * L] = jnp.ones((L, L), BF16)
    anti[...] = flag(i + j == L - 1)
    xmask[...] = flag(j >= i)
    ymask[...] = flag(j <= i)
    load.wait()

    @pl.when(working)
    def _():
        compute(
            arrived, give, (me, r, nq * nr, valid), out_ref, ones, anti, xmask, ymask,
            xf, y0, y1, sums, xs, ys0, ys1, rb, r1, r2,
            xtot, xscale, ytot0, yscale0, ytot1, yscale1,
            lhs_even, lhs_odd, fcol, ha0, ha1, hb0, hb1, na0, na1, nb0, nb1, se0, se1, so0, so1, sz0, sz1, racc0, racc1, racc2, racc3, col0, col1,
        )

    @pl.when(jnp.logical_not(working))
    def _():
        out_ref[...] = jnp.full((rows, L), -1.0, F32)

    for n in (4, 5):
        arrived(n)

        @pl.when(above)
        def _():
            out_ref[...] = jnp.maximum(out_ref[...], (got0, got1)[n - 4][...])

    for c, p in zip(copies, plan):
        pl.when(p[3])(c.wait_send)


def compute(
    arrived, give, place, out_ref, ones, anti, xmask, ymask,
    xf, y0, y1, sums, xs, ys0, ys1, rb, r1, r2,
    xtot, xscale, ytot0, yscale0, ytot1, yscale1,
    lhs_even, lhs_odd, fcol, ha0, ha1, hb0, hb1, na0, na1, nb0, nb1, se0, se1, so0, so1, sz0, sz1, racc0, racc1, racc2, racc3, col0, col1,
):
    me, r, count, valid = place
    rows = out_ref.shape[0]
    tiles = rows // 4

    slot = lax.broadcasted_iota(jnp.int32, (8, L), 0)
    lane = lax.broadcasted_iota(jnp.int32, (8, L), 1)
    parts = lambda v: [p.astype(F32) for p in split3(v)]

    def prepare(t, carry):
        own_blocks(xs, t, xmask, lhs_even, lhs_odd)
        for i in range(4):
            mean = jnp.broadcast_to(xtot[pl.ds(4 * t + i, 1), :] * (-1.0 / M), (8, L))
            hi, mid, low = parts(mean)
            window = me * (rows * L) + TILE * t + L * i + lane
            bias = jnp.where(jnp.logical_and(slot == 6, window >= valid), -BIG, 0.0)
            cols = jnp.where(slot < 3, hi, jnp.where(slot < 5, mid, jnp.where(slot < 6, low, bias)))
            cols = jnp.transpose(jnp.concatenate([cols, jnp.zeros((L - 8, L), F32)], axis=0))
            lhs = lhs_odd if i % 2 else lhs_even
            lhs[t, L * (i // 2) : L * (i // 2) + L, 3 * L : 4 * L] = cols.astype(BF16)
            scale = xscale[pl.ds(4 * t + i, 1), :]
            fcol[t, L * i : L * i + L, :] = jnp.transpose(jnp.broadcast_to(scale, (L, L)))
        middle = xs[pl.ds(16 * t + 2, 8), :]
        empty = jnp.zeros((8, L), F32)
        first = jnp.concatenate([middle, empty], axis=0).astype(BF16)
        second = jnp.concatenate([empty, middle], axis=0).astype(BF16)
        none = jnp.zeros((16, L), BF16)
        for k, v in enumerate((first, second, none, none)):
            lhs_even[t, 256:272, L * k : L * k + L] = v
        for k, v in enumerate((none, none, first, none)):
            lhs_even[t, 272:288, L * k : L * k + L] = v
            lhs_odd[t, 256:272, L * k : L * k + L] = v
        return carry

    early = tiles - 2

    def query(lo, hi):
        centre_tiles(xf, xs, sums, lo, hi)
        window_stats(xs, ones, rb, r1, r2, xtot, xscale, lo, hi)
        part = slice(16 * lo, 16 * hi)
        xs[part] = jnp.dot(xs[part].astype(BF16), anti[...], preferred_element_type=F32)
        lax.fori_loop(lo, hi, prepare, 0)

    query(0, early)
    for n in range(1, 4):
        arrived(n)
    y1[rows : rows + 8] = jnp.where(r >= 1, y0[0:8], xf[0:8])
    for y, ys, ytot, yscale in ((y0, ys0, ytot0, yscale0), (y1, ys1, ytot1, yscale1)):
        centre_tiles(y, ys, sums, 0, tiles)
        window_stats(ys, ones, rb, r1, r2, ytot, yscale, 0, tiles)

    for ref in (na0, na1, nb0, nb1):
        ref[...] = jnp.zeros((L, TILE), BF16)

    def build(job, quarter):
        t, ys, ytot, h, n = job
        shear(ys, 16 * t, h, ymask, (2 * quarter, 2 * quarter + 1))
        j = quarter
        hi, mid, low = parts(jnp.broadcast_to(ytot[pl.ds(4 * t + j, 1), :], (8, L)))
        v = jnp.where(slot == 1, mid, jnp.where(slot == 2, low, jnp.where(slot == 4, mid, hi)))
        v = jnp.where(slot < 6, v, jnp.where(slot == 6, 1.0, 0.0))
        v = jnp.concatenate([v, jnp.zeros((8, L), F32)], axis=0)
        n[0:16, L * j : L * j + L] = v.astype(BF16)

    def products(job, odd):
        t, h, n, (se, so, sz) = job
        dot = functools.partial(jnp.dot, preferred_element_type=F32)
        block = lambda k: h[:, L * k : L * k + TILE]
        last = n[...]
        if odd:
            so[...] = dot(lhs_odd[t], jnp.concatenate([block(0), block(7), block(6), last], axis=0))
        else:
            se[...] = dot(lhs_even[t], jnp.concatenate([block(0), block(7), block(1), last], axis=0))
            sz[...] = dot(lhs_even[t, 256:272, 0:L], h[:, 5 * L : 6 * L])

    def middle(sums, row, m):
        se, so, sz = sums
        if m < 4:
            v = se[256 + row : 257 + row, L * m : L * m + L]
        elif m == 4:
            v = se[272 + row : 273 + row, 3 * L : 4 * L]
        elif m == 5:
            v = sz[row : row + 1, :]
        elif m == 6:
            v = so[256 + row : 257 + row, 0:L]
        else:
            v = se[264 + row : 265 + row, L * (m - 7) : L * (m - 7) + L]
        return jnp.broadcast_to(v, (8, L))

    def maxima(job, half, state, groups):
        t, sums, yscale, col, racc, first = job
        if "scale" not in state:
            state["scale"] = [
                jnp.broadcast_to(yscale[pl.ds(4 * t + j, 1), :], (8, L)) for j in range(4)
            ]
            state["best"] = [None] * 4
        scale, best = state["scale"], state["best"]
        if ("shared", half) not in state:
            shared = []
            for e in range(-2, 4):
                v = [middle(sums, 2 * half + k - 2, k + e) for k in range(2, 8)]
                shared.append((v[0] + v[1]) + (v[2] + v[3]) + (v[4] + v[5]))
            state["shared", half] = shared
        shared = state["shared", half]
        for g in groups:
            turn = [pltpu.roll(c, 8 * g, 1, stride=1, stride_axis=0) for c in shared]
            mask = lane >= slot + 8 * g
            slid = [jnp.where(mask, turn[e + 1], turn[e]) for e in range(5)]
            for odd, s in ((0, sums[0]), (1, sums[1])):
                part = pl.ds(L * half + 8 * g, 8)
                place = pl.ds(L * (2 * half + odd) + 8 * g, 8)
                factor = fcol[t, place, :]
                row = None if first else racc[place, :]
                for j in range(4):
                    v = s[part, L * j : L * j + L] + slid[j - odd + 1]
                    a = v * scale[j]
                    row = a if row is None else jnp.maximum(row, a)
                    b = v * factor
                    best[j] = b if best[j] is None else jnp.maximum(best[j], b)
                racc[place, :] = row

    def close(job, state):
        t, _, yscale, col, _, _ = job
        for j in range(4):
            top = jnp.max(state["best"][j], axis=0, keepdims=True)
            col[pl.ds(4 * t + j, 1), :] = jnp.maximum(top * yscale[pl.ds(4 * t + j, 1), :], -1.0)

    def finish(t, racc, i):
        top = jnp.max(jnp.transpose(racc[L * i : L * i + L, :]), axis=0, keepdims=True)
        out_ref[pl.ds(4 * t + i, 1), :] = top * xscale[pl.ds(4 * t + i, 1), :]

    def step(product, top, job, rows_of=None, between=None):
        state = {}
        for quarter in range(4):
            half = quarter // 2
            if quarter % 2 == 0 and product is not None:
                products(product, half)
            maxima(top, half, state, range(8 * (quarter % 2), 8 * (quarter % 2) + 8))
            if job is not None:
                build(job, quarter)
            if rows_of is not None:
                finish(*rows_of, quarter)
            if quarter == 1 and between is not None:
                between()
        close(top, state)

    matrices = ((ha0, na0), (ha1, na1), (hb0, nb0), (hb1, nb1))
    outputs = ((se0, so0, sz0), (se1, so1, sz1))
    queries = ((ys1, ytot1, yscale1, col1), (ys0, ytot0, yscale0, col0))
    raccs = (racc0, racc1, racc2, racc3)

    def tile_of(t, k):
        return t + k % GROUP if k < 2 * GROUP else lax.rem(t + GROUP + k % GROUP, tiles)

    def matrix_job(t, k):
        ys, ytot = queries[k // GROUP % 2][:2]
        return (tile_of(t, k), ys, ytot, *matrices[k % 4])

    def product_job(t, k):
        return (tile_of(t, k), *matrices[k % 4], outputs[k % 2])

    def maxima_job(t, k):
        which = k // GROUP % 2
        return (tile_of(t, k), outputs[k % 2], *queries[which][2:], raccs[k % GROUP], which == 0)

    racc3[...] = jnp.zeros((TILE, L), F32)
    for quarter in range(4):
        build(matrix_job(0, 0), quarter)
    for odd in range(2):
        products(product_job(0, 0), odd)
    for k in (1, 2):
        for quarter in range(4):
            build(matrix_job(0, k), quarter)

    def group(t, final):
        for k in range(2 * GROUP):
            done = None
            if k == 0:
                done = (lax.rem(t + tiles - 1, tiles), raccs[GROUP - 1])
            elif k > GROUP:
                done = (t + k - GROUP - 1, raccs[k - GROUP - 1])
            between = None
            if k == GROUP:
                between = lambda: give(t, GROUP, 5)
            elif k == GROUP + 2:
                between = lambda: give(t, 2, 4)
            following = None if final and k + 1 >= 2 * GROUP else product_job(t, k + 1)
            later = None if final and k + 3 >= 2 * GROUP else matrix_job(t, k + 3)
            step(following, maxima_job(t, k), later, done, between)

    for t in range(0, tiles - GROUP, GROUP):
        if t > 0:
            give(t - 2, 2, 4)
        group(t, False)
    give(tiles - GROUP - 2, 2, 4)
    arrived(0)

    @pl.when(me == count - 1)
    def _():
        xf[rows : rows + 8] = jnp.zeros((8, L), F32)

    query(early, tiles)
    group(tiles - GROUP, True)
    give(tiles - 2, 2, 4)
    for i in range(4):
        finish(tiles - 1, racc3, i)
    cell = lax.broadcasted_iota(jnp.int32, (rows, L), 0) * L
    cell = cell + lax.broadcasted_iota(jnp.int32, (rows, L), 1)
    keep = me * (rows * L) + cell < valid
    out_ref[...] = jnp.where(keep, jnp.maximum(out_ref[...], -1.0), -1.0)


def per_device(series):
    rows = series.shape[0] // L
    tiles = rows // 4
    vm = pltpu.VMEM
    seq = vm((rows + 8, L), F32)
    cut = vm((16 * tiles, L), F32)
    sums = vm((16 * tiles, 3 * L), F32)
    line = vm((rows, L), F32)
    wide = vm((L, 11 * L), BF16)
    slots = vm((L, TILE), BF16)
    out = pl.pallas_call(
        kernel,
        out_shape=jax.ShapeDtypeStruct((rows, L), F32),
        in_specs=[pl.BlockSpec(memory_space=pltpu.HBM)],
        out_specs=pl.BlockSpec(memory_space=vm),
        scratch_shapes=[
            vm((L, 3 * L), BF16), vm((L, L), BF16), vm((L, L), BF16), vm((L, L), BF16),
            seq, seq, seq, seq, cut, cut, cut, sums, sums, sums,
            line, line, line, line, line, line,
            vm((tiles, 288, TILE), BF16), vm((tiles, 272, TILE), BF16), vm((tiles, TILE, L), F32),
            wide, wide, wide, wide, slots, slots, slots, slots,
            vm((288, TILE), F32), vm((288, TILE), F32), vm((272, TILE), F32), vm((272, TILE), F32),
            vm((16, L), F32), vm((16, L), F32), vm((TILE, L), F32), vm((TILE, L), F32),
            vm((TILE, L), F32), vm((TILE, L), F32),
            line, line, line, line,
            pltpu.SemaphoreType.DMA((6,)), pltpu.SemaphoreType.DMA((6,)),
            pltpu.SemaphoreType.DMA,
        ],
        compiler_params=pltpu.CompilerParams(
            collective_id=0, has_side_effects=True, vmem_limit_bytes=48 * 2**20
        ),
    )(pltpu.with_memory_space_constraint(series.reshape(rows, L), pltpu.HBM))
    return out.reshape(-1)


def solution(mesh):
    placed = (P(("qry", "ref")),)
    return jax.shard_map(
        per_device, mesh=mesh, in_specs=placed, out_specs=P(("qry", "ref")), check_vma=False
    )
```
